512 devices in a mesh: grp: 16 (over y, core), dev: 32 (over x, z).
Axes of the slice: x: 4, y: 8, z: 8, core: 2. Of those that a mesh axis runs over, the one named last changes fastest.
Arguments:
- wave: bfloat16 [16384, 384], P(('grp', 'dev')), may hold values from -6 to 6
- lengths: int32 [16384], P('grp'), may hold values from 288 to 384, as said below
- order: int32 [512, 32], P('grp'), may hold values from 0 to 31, each once within a row
- w_first: bfloat16 [10, 512], replicated, may hold values from -2 to 2
- norm_gain: float32 [512], replicated, may hold values from 0.1 to 1.9
- norm_bias: float32 [512], replicated, may hold values from -3 to 3
- w_second: bfloat16 [3, 512, 512], replicated, may hold values from -0.15625 to 0.15625
- cot: bfloat16 [16384, 37, 512], P(('grp', 'dev')), may hold values from -0.0234375 to 0.0234375
Outputs:
- features: bfloat16 [16384, 37, 512], P(('grp', 'dev'))
- grad_second: float32 [3, 512, 512], P(None, None, 'dev')
- grad_first: float32 [10, 512], P(None, 'dev')
- grad_gain: float32 [512], P('dev')
- grad_bias: float32 [512], P('dev')
The draws below stay inside these ranges and needn't reach their ends.
Inputs may be any that keep to these rules, and one draw needn't show every extreme that they name: `lengths`: every aligned block of 32 rows (the rows of one device) holds a row of exactly 384 valid samples. Each row of order is a permutation of 0 .. 31.
All inputs are finite; a program needn't handle non-finite values.
Results may differ from the reference program's by a relative error of at most 0.0054.
Values may be sent and summed in bfloat16 or wider, within the bound.
A program may use at most 64 MiB of HBM per device.

```python
import jax
import jax.numpy as jnp
from jax import lax

CH = 512
K0 = 10
K1 = 3
ROW_DEV = 32
SAMP = 384
MINLEN = 288
F1 = 37
ROWS = 16384
N_GRP = 16
N_DEV = 32
DEVICES = 512


def draw_lengths(key, part):
    first, second = jax.random.split(jax.random.fold_in(key, 17))
    blocks = ROWS // ROW_DEV
    values = jax.random.randint(first, (blocks, ROW_DEV), MINLEN, SAMP + 1, dtype=jnp.int32)
    where_full = jax.random.randint(second, (blocks, 1), 0, ROW_DEV, dtype=jnp.int32)
    column = jnp.arange(ROW_DEV, dtype=jnp.int32)[None, :]
    values = jnp.where(column == where_full, SAMP, values)
    return values.reshape(ROWS).astype(jnp.int32)


def levels(stream_key, extent, cuts, least, top_value):
    factor_of = 1.0
    for position, shards_of in cuts:
        steps = jax.random.uniform(jax.random.fold_in(jax.random.fold_in(stream_key, 6), position), (shards_of,), jnp.float32, least / len(cuts), top_value / len(cuts))
        factor_of = factor_of * jnp.repeat(jnp.exp(steps), extent[position] // shards_of).reshape((-1,) + (1,) * (len(extent) - 1 - position))
    return factor_of


def noise(own_key, shape, width, most, cuts=(), kind=jnp.bfloat16):
    loudness = levels(own_key, shape, cuts, -0.22, 0.18) if cuts else 1.0
    array = jax.random.normal(own_key, shape, jnp.float32) * width * loudness
    return jnp.minimum(jnp.maximum(array, -most), most).astype(kind)


def setup_inputs(seed: int = 0) -> dict:
    streams_of = jax.random.split(jax.random.key(seed), 9)
    wave = noise(streams_of[0], (ROWS, SAMP), 1.0, 6.0, ((0, 512),))
    lengths = draw_lengths(jax.random.fold_in(streams_of[8], 71), 0)
    order = jax.vmap(lambda own: jax.random.permutation(own, ROW_DEV))(jax.random.split(streams_of[2], DEVICES)).reshape((DEVICES, ROW_DEV)).astype(jnp.int32)
    w_first = noise(streams_of[3], (K0, CH), K0 ** -0.5, 2.0)
    norm_gain = jnp.clip(1.0 + 0.18 * jax.random.normal(streams_of[4], (CH,), jnp.float32), 0.1, 1.9)
    norm_bias = noise(streams_of[5], (CH,), 0.5, 3.0, (), jnp.float32)
    w_second = noise(streams_of[6], (K1, CH, CH), (K1 * CH) ** -0.5, 0.15625)
    cot = noise(streams_of[7], (ROWS, F1, CH), 0.004, 0.0234375, ((0, 512),))
    return dict(wave=wave, lengths=lengths, order=order, w_first=w_first, norm_gain=norm_gain, norm_bias=norm_bias, w_second=w_second, cot=cot)


def gelu_slope(value):
    return 0.5 * (1.0 + lax.erf(value * 0.7071067811865476)) + value * jnp.exp(-0.5 * value * value) * 0.3989422804014327

def local_pass(wave, lens, w_first, norm_gain, norm_bias, w_second, cot):
    rows, samp = wave.shape
    ker_first = w_first.shape[0]
    stride_first = ker_first // 2
    chans = w_first.shape[1]
    taps_second = w_second.shape[0]
    frames0 = (samp - ker_first) // stride_first + 1
    frames1 = (frames0 - taps_second) // 2 + 1
    blocks = wave[:, :stride_first * (frames0 + 1)].reshape(rows, frames0 + 1, stride_first)
    patches = jnp.concatenate([blocks[:, :-1], blocks[:, 1:]], axis=2).reshape(rows * frames0, ker_first)
    pre0 = jnp.dot(patches, w_first, preferred_element_type=jnp.float32).reshape(rows, frames0, chans)
    valid0 = (lens - ker_first) // stride_first + 1
    mask0 = (jnp.arange(frames0, dtype=jnp.int32)[None, :] < valid0[:, None]).astype(jnp.float32)[:, :, None]
    count0 = valid0.astype(jnp.float32)[:, None, None]
    mean0 = lax.optimization_barrier(jnp.sum(pre0 * mask0, axis=1, keepdims=True)) / count0
    centred = (pre0 - mean0) * mask0
    var0 = lax.optimization_barrier(jnp.sum(centred * centred, axis=1, keepdims=True)) / count0
    inv_std = lax.rsqrt(var0 + 1e-05)
    normed = centred * inv_std
    lifted = normed * norm_gain + norm_bias
    act0 = (jax.nn.gelu(lifted, approximate=False) * mask0).astype(jnp.bfloat16)
    span = 2 * frames1
    taps = jnp.concatenate([act0[:, 0:span:2], act0[:, 1:span:2], act0[:, 2:span + 1:2]], axis=2)
    taps = taps.reshape(rows * frames1, taps_second * chans)
    kernel = w_second.reshape(taps_second * chans, chans)
    pre1 = jnp.dot(taps, kernel, preferred_element_type=jnp.float32).reshape(rows, frames1, chans)
    valid1 = (valid0 - taps_second) // 2 + 1
    mask1 = (jnp.arange(frames1, dtype=jnp.int32)[None, :] < valid1[:, None]).astype(jnp.float32)[:, :, None]
    features = (jax.nn.gelu(pre1, approximate=False) * mask1).astype(jnp.bfloat16)
    grad1 = (cot.astype(jnp.float32) * gelu_slope(pre1) * mask1).astype(jnp.bfloat16).reshape(rows * frames1, chans)
    grad_kernel = lax.dot_general(taps, grad1, (((0,), (0,)), ((), ())), preferred_element_type=jnp.float32)
    back = lax.dot_general(grad1, kernel, (((1,), (1,)), ((), ())), preferred_element_type=jnp.float32)
    back = back.reshape(rows, frames1, taps_second, chans)
    zero_row = jnp.zeros((rows, 1, chans), jnp.float32)
    even = back[:, :, 0] + jnp.concatenate([zero_row, back[:, :-1, 2]], axis=1)
    odd = back[:, :, 1]
    pieces = [jnp.stack([even, odd], axis=2).reshape(rows, span, chans), back[:, -1:, 2]]
    if frames0 > span + 1:
        pieces.append(jnp.zeros((rows, frames0 - span - 1, chans), jnp.float32))
    dact0 = jnp.concatenate(pieces, axis=1)
    dlift = dact0 * gelu_slope(lifted) * mask0
    grad_gain = lax.optimization_barrier(jnp.sum(dlift * normed, axis=(0, 1)))
    grad_bias = lax.optimization_barrier(jnp.sum(dlift, axis=(0, 1)))
    dnorm = dlift * norm_gain
    first_mean = lax.optimization_barrier(jnp.sum(dnorm, axis=1, keepdims=True)) / count0
    second_mean = lax.optimization_barrier(jnp.sum(dnorm * normed, axis=1, keepdims=True)) / count0
    dpre0 = inv_std * (dnorm - first_mean - normed * second_mean) * mask0
    grad_filter = lax.dot_general(patches.astype(jnp.float32), dpre0.reshape(rows * frames0, chans), (((0,), (0,)), ((), ())), precision=lax.Precision.HIGHEST, preferred_element_type=jnp.float32)
    grads = jnp.concatenate([grad_kernel, grad_filter, grad_gain[None, :], grad_bias[None, :]], axis=0)
    return (features, grads)

def reference(wave, lengths, order, w_first, norm_gain, norm_bias, w_second, cot):
    groups = N_GRP
    members = N_DEV
    share = ROW_DEV // members
    samp = wave.shape[1]
    shaped = wave.reshape(groups, members, ROW_DEV, samp)
    picks = order.reshape(groups, members, ROW_DEV)
    picked = jnp.take_along_axis(shaped, picks[..., None], axis=2)
    moved = picked.reshape(groups, members, share, members, samp).transpose(0, 3, 1, 2, 4).reshape(groups * members, ROW_DEV, samp)
    lens = jnp.take_along_axis(lengths.reshape(groups, members, ROW_DEV), picks, axis=2)
    lens = lens.reshape(groups, members, share, members).transpose(0, 3, 1, 2).reshape(groups * members, ROW_DEV)
    cots = cot.reshape(groups * members, ROW_DEV, F1, CH)

    def step(total, block):
        feats, grads = local_pass(block[0], block[1], w_first, norm_gain, norm_bias, w_second, block[2])
        return (total + grads, feats)
    init = jnp.zeros((K1 * CH + K0 + 2, CH), jnp.float32)
    total, feats = lax.scan(step, init, (moved, lens, cots))
    features = feats.reshape(ROWS, F1, CH)
    grad_second = total[:K1 * CH].reshape(K1, CH, CH)
    grad_first = total[K1 * CH:K1 * CH + K0]
    grad_gain = total[K1 * CH + K0]
    grad_bias = total[K1 * CH + K0 + 1]
    return (features, grad_second, grad_first, grad_gain, grad_bias)
```

```python
import jax
import jax.numpy as jnp
from jax import lax
from jax.sharding import PartitionSpec as P


def gelu_slope(value):
    return (
        0.5 * (1.0 + lax.erf(value * 0.7071067811865476))
        + value * jnp.exp(-0.5 * value * value) * 0.3989422804014327
    )


def local_pass(wave, lens, w_first, norm_gain, norm_bias, w_second, cot):
    rows, samp = wave.shape
    ker_first = w_first.shape[0]
    stride_first = ker_first // 2
    chans = w_first.shape[1]
    taps_second = w_second.shape[0]
    frames0 = (samp - ker_first) // stride_first + 1
    frames1 = (frames0 - taps_second) // 2 + 1
    blocks = wave[:, : stride_first * (frames0 + 1)].reshape(rows, frames0 + 1, stride_first)
    patches = jnp.concatenate([blocks[:, :-1], blocks[:, 1:]], axis=2).reshape(
        rows * frames0, ker_first
    )
    pre0 = jnp.dot(patches, w_first, preferred_element_type=jnp.float32).reshape(
        rows, frames0, chans
    )
    valid0 = (lens - ker_first) // stride_first + 1
    mask0 = (jnp.arange(frames0, dtype=jnp.int32)[None, :] < valid0[:, None]).astype(jnp.float32)[
        :, :, None
    ]
    count0 = valid0.astype(jnp.float32)[:, None, None]
    mean0 = jnp.sum(pre0 * mask0, axis=1, keepdims=True) / count0
    centred = (pre0 - mean0) * mask0
    var0 = jnp.sum(centred * centred, axis=1, keepdims=True) / count0
    inv_std = lax.rsqrt(var0 + 1e-05)
    normed = centred * inv_std
    lifted = normed * norm_gain + norm_bias
    act0 = (jax.nn.gelu(lifted, approximate=False) * mask0).astype(jnp.bfloat16)
    span = 2 * frames1
    taps = jnp.concatenate(
        [act0[:, 0:span:2], act0[:, 1:span:2], act0[:, 2 : span + 1 : 2]], axis=2
    )
    taps = taps.reshape(rows * frames1, taps_second * chans)
    kernel = w_second.reshape(taps_second * chans, chans)
    pre1 = jnp.dot(taps, kernel, preferred_element_type=jnp.float32).reshape(rows, frames1, chans)
    valid1 = (valid0 - taps_second) // 2 + 1
    mask1 = (jnp.arange(frames1, dtype=jnp.int32)[None, :] < valid1[:, None]).astype(jnp.float32)[
        :, :, None
    ]
    features = (jax.nn.gelu(pre1, approximate=False) * mask1).astype(jnp.bfloat16)
    grad1 = (
        (cot.astype(jnp.float32) * gelu_slope(pre1) * mask1)
        .astype(jnp.bfloat16)
        .reshape(rows * frames1, chans)
    )
    grad_kernel = lax.dot_general(
        grad1, taps, (((0,), (0,)), ((), ())), preferred_element_type=jnp.float32
    )
    back = lax.dot_general(
        grad1, kernel, (((1,), (1,)), ((), ())), preferred_element_type=jnp.float32
    )
    back = back.reshape(rows, frames1, taps_second, chans)
    zero_row = jnp.zeros((rows, 1, chans), jnp.float32)
    even = back[:, :, 0] + jnp.concatenate([zero_row, back[:, :-1, 2]], axis=1)
    odd = back[:, :, 1]
    pieces = [jnp.stack([even, odd], axis=2).reshape(rows, span, chans), back[:, -1:, 2]]
    dact0 = jnp.concatenate(pieces, axis=1)
    dlift = dact0 * gelu_slope(lifted) * mask0
    grad_gain = jnp.sum(dlift * normed, axis=(0, 1))
    grad_bias = jnp.sum(dlift, axis=(0, 1))
    dnorm = dlift * norm_gain
    first_mean = jnp.sum(dnorm, axis=1, keepdims=True) / count0
    second_mean = jnp.sum(dnorm * normed, axis=1, keepdims=True) / count0
    dpre0 = inv_std * (dnorm - first_mean - normed * second_mean) * mask0
    grad_filter = lax.dot_general(
        dpre0.reshape(rows * frames0, chans),
        patches.astype(jnp.float32),
        (((0,), (0,)), ((), ())),
        precision=lax.Precision.HIGHEST,
        preferred_element_type=jnp.float32,
    )
    small = jnp.concatenate([grad_filter, grad_gain[:, None], grad_bias[:, None]], axis=1)
    grads = (grad_kernel, small)
    return (features, grads)


def shards(wave, lengths, order, w_first, norm_gain, norm_bias, w_second, cot):
    members = lax.axis_size("dev")
    member = lax.axis_index("dev")
    rows = wave.shape[0]
    share = rows // members
    own_order = lax.dynamic_index_in_dim(order, member, 0, keepdims=False)
    dealt = own_order.reshape(share, members).T.reshape(rows)
    outgoing = jnp.take(wave, dealt, axis=0)
    arrived = lax.all_to_all(outgoing, "dev", split_axis=0, concat_axis=0, tiled=True)
    group_lens = jnp.take_along_axis(lengths.reshape(members, rows), order, axis=1)
    group_lens = group_lens.reshape(members, share, members)
    lens = lax.dynamic_index_in_dim(group_lens, member, 2, keepdims=False).reshape(rows)
    features, (grad_kernel, small) = local_pass(
        arrived, lens, w_first, norm_gain, norm_bias, w_second, cot
    )
    taps_second = w_second.shape[0]
    in_chans = w_second.shape[1]
    part_kernel = lax.psum_scatter(grad_kernel, "dev", scatter_dimension=0, tiled=True)
    part_small = lax.psum_scatter(small, "dev", scatter_dimension=0, tiled=True)
    owned_kernel = lax.psum(part_kernel, "grp")
    owned_small = lax.psum(part_small, "grp")
    width = owned_kernel.shape[0]
    grad_second = owned_kernel.reshape(width, taps_second, in_chans).transpose(1, 2, 0)
    ker_first = w_first.shape[0]
    grad_first = owned_small[:, :ker_first].T
    grad_gain = owned_small[:, ker_first]
    grad_bias = owned_small[:, ker_first + 1]
    return (features, grad_second, grad_first, grad_gain, grad_bias)


def solution(mesh):
    placed = (
        P(("grp", "dev"), None),
        P("grp"),
        P("grp", None),
        P(),
        P(),
        P(),
        P(),
        P(("grp", "dev"), None, None),
    )
    return jax.shard_map(
        shards,
        mesh=mesh,
        in_specs=placed,
        out_specs=(
            P(("grp", "dev"), None, None),
            P(None, None, "dev"),
            P(None, "dev"),
            P("dev"),
            P("dev"),
        ),
        check_vma=False,
    )
```

```python
import jax
import jax.numpy as jnp
from jax import lax
from jax.sharding import PartitionSpec as P


def gelu_slope(value):
    return (
        0.5 * (1.0 + lax.erf(value * 0.7071067811865476))
        + value * jnp.exp(-0.5 * value * value) * 0.3989422804014327
    )


def local_pass(wave, lens, w_first, norm_gain, norm_bias, w_second, cot):
    rows, samp = wave.shape
    ker_first = w_first.shape[0]
    stride_first = ker_first // 2
    chans = w_first.shape[1]
    taps_second = w_second.shape[0]
    frames0 = (samp - ker_first) // stride_first + 1
    frames1 = (frames0 - taps_second) // 2 + 1
    blocks = wave[:, : stride_first * (frames0 + 1)].reshape(rows, frames0 + 1, stride_first)
    patches = jnp.concatenate([blocks[:, :-1], blocks[:, 1:]], axis=2).reshape(
        rows * frames0, ker_first
    )
    pre0 = jnp.dot(patches, w_first, preferred_element_type=jnp.float32).reshape(
        rows, frames0, chans
    )
    valid0 = (lens - ker_first) // stride_first + 1
    mask0 = (jnp.arange(frames0, dtype=jnp.int32)[None, :] < valid0[:, None]).astype(jnp.float32)[
        :, :, None
    ]
    count0 = valid0.astype(jnp.float32)[:, None, None]
    mean0 = jnp.sum(pre0 * mask0, axis=1, keepdims=True) / count0
    centred = (pre0 - mean0) * mask0
    var0 = jnp.sum(centred * centred, axis=1, keepdims=True) / count0
    inv_std = lax.rsqrt(var0 + 1e-05)
    normed = centred * inv_std
    lifted = normed * norm_gain + norm_bias
    act0 = (jax.nn.gelu(lifted, approximate=False) * mask0).astype(jnp.bfloat16)
    span = 2 * frames1
    taps = jnp.concatenate(
        [act0[:, 0:span:2], act0[:, 1:span:2], act0[:, 2 : span + 1 : 2]], axis=2
    )
    taps = taps.reshape(rows * frames1, taps_second * chans)
    kernel = w_second.reshape(taps_second * chans, chans)
    pre1 = jnp.dot(taps, kernel, preferred_element_type=jnp.float32).reshape(rows, frames1, chans)
    valid1 = (valid0 - taps_second) // 2 + 1
    mask1 = (jnp.arange(frames1, dtype=jnp.int32)[None, :] < valid1[:, None]).astype(jnp.float32)[
        :, :, None
    ]
    features = (jax.nn.gelu(pre1, approximate=False) * mask1).astype(jnp.bfloat16)
    grad1 = (
        (cot.astype(jnp.float32) * gelu_slope(pre1) * mask1)
        .astype(jnp.bfloat16)
        .reshape(rows * frames1, chans)
    )
    grad_kernel = lax.dot_general(
        grad1, taps, (((0,), (0,)), ((), ())), preferred_element_type=jnp.float32
    )
    back = lax.dot_general(
        grad1, kernel, (((1,), (1,)), ((), ())), preferred_element_type=jnp.float32
    )
    back = back.reshape(rows, frames1, taps_second, chans)
    zero_row = jnp.zeros((rows, 1, chans), jnp.float32)
    even = back[:, :, 0] + jnp.concatenate([zero_row, back[:, :-1, 2]], axis=1)
    odd = back[:, :, 1]
    pieces = [jnp.stack([even, odd], axis=2).reshape(rows, span, chans), back[:, -1:, 2]]
    dact0 = jnp.concatenate(pieces, axis=1)
    dlift = dact0 * gelu_slope(lifted) * mask0
    grad_gain = jnp.sum(dlift * normed, axis=(0, 1))
    grad_bias = jnp.sum(dlift, axis=(0, 1))
    dnorm = dlift * norm_gain
    first_mean = jnp.sum(dnorm, axis=1, keepdims=True) / count0
    second_mean = jnp.sum(dnorm * normed, axis=1, keepdims=True) / count0
    dpre0 = inv_std * (dnorm - first_mean - normed * second_mean) * mask0
    grad_filter = lax.dot_general(
        dpre0.reshape(rows * frames0, chans),
        patches.astype(jnp.float32),
        (((0,), (0,)), ((), ())),
        precision=lax.Precision.HIGHEST,
        preferred_element_type=jnp.float32,
    )
    small = jnp.concatenate([grad_filter, grad_gain[:, None], grad_bias[:, None]], axis=1)
    grads = (grad_kernel, small)
    return (features, grads)


def shards(wave, lengths, order, w_first, norm_gain, norm_bias, w_second, cot):
    members = lax.axis_size("dev")
    member = lax.axis_index("dev")
    rows = wave.shape[0]
    share = rows // members
    own_order = lax.dynamic_index_in_dim(order, member, 0, keepdims=False)
    dealt = own_order.reshape(share, members).T.reshape(rows)
    outgoing = jnp.take(wave, dealt, axis=0)
    arrived = lax.all_to_all(outgoing, "dev", split_axis=0, concat_axis=0, tiled=True)
    group_lens = jnp.take_along_axis(lengths.reshape(members, rows), order, axis=1)
    group_lens = group_lens.reshape(members, share, members)
    lens = lax.dynamic_index_in_dim(group_lens, member, 2, keepdims=False).reshape(rows)
    features, (grad_kernel, small) = local_pass(
        arrived, lens, w_first, norm_gain, norm_bias, w_second, cot
    )
    taps_second = w_second.shape[0]
    in_chans = w_second.shape[1]
    ker_first = w_first.shape[0]
    members = lax.axis_size("dev")
    groups = lax.axis_size("grp")
    full = jnp.concatenate([grad_kernel, small], axis=1)
    chans, span = full.shape
    width = chans // members
    pieces = lax.all_to_all(
        full.reshape(members, width, span), "dev", split_axis=0, concat_axis=0, tiled=True
    )
    part = jnp.sum(pieces, axis=0)
    sub = width // groups
    mine = lax.all_to_all(
        part.reshape(groups, sub, span), "grp", split_axis=0, concat_axis=0, tiled=True
    )
    mine = jnp.sum(mine, axis=0)
    spread = jnp.broadcast_to(mine[None], (groups, sub, span))
    owned = lax.all_to_all(spread, "grp", split_axis=0, concat_axis=0, tiled=True)
    owned = owned.reshape(width, span)
    grad_second = (
        owned[:, : taps_second * in_chans].reshape(width, taps_second, in_chans).transpose(1, 2, 0)
    )
    grad_first = owned[:, taps_second * in_chans : taps_second * in_chans + ker_first].T
    grad_gain = owned[:, taps_second * in_chans + ker_first]
    grad_bias = owned[:, taps_second * in_chans + ker_first + 1]
    return (features, grad_second, grad_first, grad_gain, grad_bias)


def solution(mesh):
    placed = (
        P(("grp", "dev"), None),
        P("grp"),
        P("grp", None),
        P(),
        P(),
        P(),
        P(),
        P(("grp", "dev"), None, None),
    )
    return jax.shard_map(
        shards,
        mesh=mesh,
        in_specs=placed,
        out_specs=(
            P(("grp", "dev"), None, None),
            P(None, None, "dev"),
            P(None, "dev"),
            P("dev"),
            P("dev"),
        ),
        check_vma=False,
    )
```

```python
import functools

import jax
import jax.numpy as jnp
from jax import lax
from jax.experimental import pallas as pl
from jax.experimental.pallas import tpu as pltpu
from jax.sharding import PartitionSpec as P

MESH = pl.DeviceIdType.MESH


def exchange_kernel(members, src_ref, dst_ref, send_sems, recv_sems, local_sem):
    me = lax.axis_index("dev")
    grp = lax.axis_index("grp")
    barrier = pltpu.get_barrier_semaphore()

    def greet(step, carry):
        peer = lax.rem(me + step, members)
        pl.semaphore_signal(barrier, inc=1, device_id=(grp, peer), device_id_type=MESH)
        return carry

    lax.fori_loop(1, members, greet, 0)
    pl.semaphore_wait(barrier, members - 1)
    local = pltpu.make_async_copy(src_ref.at[me], dst_ref.at[me], local_sem)
    local.start()

    def send(step, carry):
        peer = lax.rem(me + step, members)
        pltpu.make_async_remote_copy(
            src_ref=src_ref.at[peer],
            dst_ref=dst_ref.at[me],
            send_sem=send_sems.at[step],
            recv_sem=recv_sems.at[step],
            device_id=(grp, peer),
            device_id_type=MESH,
        ).start()
        return carry

    lax.fori_loop(1, members, send, 0)

    def finish(step, carry):
        peer = lax.rem(me + step, members)
        sender = lax.rem(me + members - step, members)
        pltpu.make_async_remote_copy(
            src_ref=src_ref.at[peer],
            dst_ref=dst_ref.at[me],
            send_sem=send_sems.at[step],
            recv_sem=recv_sems.at[step],
            device_id=(grp, peer),
            device_id_type=MESH,
        ).wait_send()
        pltpu.make_async_remote_copy(
            src_ref=src_ref.at[me],
            dst_ref=dst_ref.at[sender],
            send_sem=send_sems.at[step],
            recv_sem=recv_sems.at[step],
            device_id=(grp, sender),
            device_id_type=MESH,
        ).wait_recv()
        return carry

    lax.fori_loop(1, members, finish, 0)
    local.wait()


def exchange(blocks):
    members = blocks.shape[0]
    return pl.pallas_call(
        functools.partial(exchange_kernel, members),
        out_shape=jax.ShapeDtypeStruct(blocks.shape, blocks.dtype),
        in_specs=[pl.BlockSpec(memory_space=pl.ANY)],
        out_specs=pl.BlockSpec(memory_space=pl.ANY),
        scratch_shapes=[
            pltpu.SemaphoreType.DMA((members,)),
            pltpu.SemaphoreType.DMA((members,)),
            pltpu.SemaphoreType.DMA,
        ],
        compiler_params=pltpu.CompilerParams(collective_id=0, has_side_effects=True),
    )(blocks)


def gelu_slope(value):
    return (
        0.5 * (1.0 + lax.erf(value * 0.7071067811865476))
        + value * jnp.exp(-0.5 * value * value) * 0.3989422804014327
    )


def local_pass(wave, lens, w_first, norm_gain, norm_bias, w_second, cot):
    rows, samp = wave.shape
    ker_first = w_first.shape[0]
    stride_first = ker_first // 2
    chans = w_first.shape[1]
    taps_second = w_second.shape[0]
    frames0 = (samp - ker_first) // stride_first + 1
    frames1 = (frames0 - taps_second) // 2 + 1
    blocks = wave[:, : stride_first * (frames0 + 1)].reshape(rows, frames0 + 1, stride_first)
    patches = jnp.concatenate([blocks[:, :-1], blocks[:, 1:]], axis=2).reshape(
        rows * frames0, ker_first
    )
    pre0 = jnp.dot(patches, w_first, preferred_element_type=jnp.float32).reshape(
        rows, frames0, chans
    )
    valid0 = (lens - ker_first) // stride_first + 1
    mask0 = (jnp.arange(frames0, dtype=jnp.int32)[None, :] < valid0[:, None]).astype(jnp.float32)[
        :, :, None
    ]
    count0 = valid0.astype(jnp.float32)[:, None, None]
    mean0 = jnp.sum(pre0 * mask0, axis=1, keepdims=True) / count0
    centred = (pre0 - mean0) * mask0
    var0 = jnp.sum(centred * centred, axis=1, keepdims=True) / count0
    inv_std = lax.rsqrt(var0 + 1e-05)
    normed = centred * inv_std
    lifted = normed * norm_gain + norm_bias
    act0 = (jax.nn.gelu(lifted, approximate=False) * mask0).astype(jnp.bfloat16)
    span = 2 * frames1
    taps = jnp.concatenate(
        [act0[:, 0:span:2], act0[:, 1:span:2], act0[:, 2 : span + 1 : 2]], axis=2
    )
    taps = taps.reshape(rows * frames1, taps_second * chans)
    kernel = w_second.reshape(taps_second * chans, chans)
    pre1 = jnp.dot(taps, kernel, preferred_element_type=jnp.float32).reshape(rows, frames1, chans)
    valid1 = (valid0 - taps_second) // 2 + 1
    mask1 = (jnp.arange(frames1, dtype=jnp.int32)[None, :] < valid1[:, None]).astype(jnp.float32)[
        :, :, None
    ]
    features = (jax.nn.gelu(pre1, approximate=False) * mask1).astype(jnp.bfloat16)
    grad1 = (
        (cot.astype(jnp.float32) * gelu_slope(pre1) * mask1)
        .astype(jnp.bfloat16)
        .reshape(rows * frames1, chans)
    )
    grad_kernel = lax.dot_general(
        grad1, taps, (((0,), (0,)), ((), ())), preferred_element_type=jnp.float32
    )
    back = lax.dot_general(
        grad1, kernel, (((1,), (1,)), ((), ())), preferred_element_type=jnp.float32
    )
    back = back.reshape(rows, frames1, taps_second, chans)
    zero_row = jnp.zeros((rows, 1, chans), jnp.float32)
    even = back[:, :, 0] + jnp.concatenate([zero_row, back[:, :-1, 2]], axis=1)
    odd = back[:, :, 1]
    pieces = [jnp.stack([even, odd], axis=2).reshape(rows, span, chans), back[:, -1:, 2]]
    dact0 = jnp.concatenate(pieces, axis=1)
    dlift = dact0 * gelu_slope(lifted) * mask0
    grad_gain = jnp.sum(dlift * normed, axis=(0, 1))
    grad_bias = jnp.sum(dlift, axis=(0, 1))
    dnorm = dlift * norm_gain
    first_mean = jnp.sum(dnorm, axis=1, keepdims=True) / count0
    second_mean = jnp.sum(dnorm * normed, axis=1, keepdims=True) / count0
    dpre0 = inv_std * (dnorm - first_mean - normed * second_mean) * mask0
    grad_filter = lax.dot_general(
        dpre0.reshape(rows * frames0, chans),
        patches.astype(jnp.float32),
        (((0,), (0,)), ((), ())),
        precision=lax.Precision.HIGHEST,
        preferred_element_type=jnp.float32,
    )
    small = jnp.concatenate([grad_filter, grad_gain[:, None], grad_bias[:, None]], axis=1)
    grads = (grad_kernel, small)
    return (features, grads)


def shards(wave, lengths, order, w_first, norm_gain, norm_bias, w_second, cot):
    members = lax.axis_size("dev")
    member = lax.axis_index("dev")
    rows = wave.shape[0]
    share = rows // members
    own_order = lax.dynamic_index_in_dim(order, member, 0, keepdims=False)
    dealt = own_order.reshape(share, members).T.reshape(rows)
    outgoing = jnp.take(wave, dealt, axis=0)
    arrived = lax.all_to_all(outgoing, "dev", split_axis=0, concat_axis=0, tiled=True)
    group_lens = jnp.take_along_axis(lengths.reshape(members, rows), order, axis=1)
    group_lens = group_lens.reshape(members, share, members)
    lens = lax.dynamic_index_in_dim(group_lens, member, 2, keepdims=False).reshape(rows)
    features, (grad_kernel, small) = local_pass(
        arrived, lens, w_first, norm_gain, norm_bias, w_second, cot
    )
    taps_second = w_second.shape[0]
    in_chans = w_second.shape[1]
    ker_first = w_first.shape[0]
    members = lax.axis_size("dev")
    groups = lax.axis_size("grp")
    full = jnp.concatenate([grad_kernel, small], axis=1)
    chans, span = full.shape
    width = chans // members
    pieces = exchange(full.reshape(members, width, span))
    part = jnp.sum(pieces, axis=0)
    sub = width // groups
    mine = lax.all_to_all(
        part.reshape(groups, sub, span), "grp", split_axis=0, concat_axis=0, tiled=True
    )
    mine = jnp.sum(mine, axis=0)
    spread = jnp.broadcast_to(mine[None], (groups, sub, span))
    owned = lax.all_to_all(spread, "grp", split_axis=0, concat_axis=0, tiled=True)
    owned = owned.reshape(width, span)
    grad_second = (
        owned[:, : taps_second * in_chans].reshape(width, taps_second, in_chans).transpose(1, 2, 0)
    )
    grad_first = owned[:, taps_second * in_chans : taps_second * in_chans + ker_first].T
    grad_gain = owned[:, taps_second * in_chans + ker_first]
    grad_bias = owned[:, taps_second * in_chans + ker_first + 1]
    return (features, grad_second, grad_first, grad_gain, grad_bias)


def solution(mesh):
    placed = (
        P(("grp", "dev"), None),
        P("grp"),
        P("grp", None),
        P(),
        P(),
        P(),
        P(),
        P(("grp", "dev"), None, None),
    )
    return jax.shard_map(
        shards,
        mesh=mesh,
        in_specs=placed,
        out_specs=(
            P(("grp", "dev"), None, None),
            P(None, None, "dev"),
            P(None, "dev"),
            P("dev"),
            P("dev"),
        ),
        check_vma=False,
    )
```

```python
import functools

import jax
import jax.numpy as jnp
from jax import lax
from jax.experimental import pallas as pl
from jax.experimental.pallas import tpu as pltpu
from jax.sharding import PartitionSpec as P

MESH = pl.DeviceIdType.MESH


def exchange_kernel(members, axis, gather, src_ref, dst_ref, send_sems, recv_sems, local_sem):
    me = lax.axis_index(axis)
    other = lax.axis_index("dev" if axis == "grp" else "grp")

    def where(peer):
        return (peer, other) if axis == "grp" else (other, peer)

    def source(peer):
        return src_ref.at[0] if gather else src_ref.at[peer]

    barrier = pltpu.get_barrier_semaphore()

    def greet(step, carry):
        peer = lax.rem(me + step, members)
        pl.semaphore_signal(barrier, inc=1, device_id=where(peer), device_id_type=MESH)
        return carry

    lax.fori_loop(1, members, greet, 0)
    pl.semaphore_wait(barrier, members - 1)
    local = pltpu.make_async_copy(source(me), dst_ref.at[me], local_sem)
    local.start()

    def send(step, carry):
        peer = lax.rem(me + step, members)
        pltpu.make_async_remote_copy(
            src_ref=source(peer),
            dst_ref=dst_ref.at[me],
            send_sem=send_sems.at[step],
            recv_sem=recv_sems.at[step],
            device_id=where(peer),
            device_id_type=MESH,
        ).start()
        return carry

    lax.fori_loop(1, members, send, 0)

    def finish(step, carry):
        peer = lax.rem(me + step, members)
        sender = lax.rem(me + members - step, members)
        pltpu.make_async_remote_copy(
            src_ref=source(peer),
            dst_ref=dst_ref.at[me],
            send_sem=send_sems.at[step],
            recv_sem=recv_sems.at[step],
            device_id=where(peer),
            device_id_type=MESH,
        ).wait_send()
        pltpu.make_async_remote_copy(
            src_ref=source(me),
            dst_ref=dst_ref.at[sender],
            send_sem=send_sems.at[step],
            recv_sem=recv_sems.at[step],
            device_id=where(sender),
            device_id_type=MESH,
        ).wait_recv()
        return carry

    lax.fori_loop(1, members, finish, 0)
    local.wait()


def exchange(blocks, members, axis, gather, ident):
    shape = (members,) + blocks.shape[1:]
    return pl.pallas_call(
        functools.partial(exchange_kernel, members, axis, gather),
        out_shape=jax.ShapeDtypeStruct(shape, blocks.dtype),
        in_specs=[pl.BlockSpec(memory_space=pl.ANY)],
        out_specs=pl.BlockSpec(memory_space=pl.ANY),
        scratch_shapes=[
            pltpu.SemaphoreType.DMA((members,)),
            pltpu.SemaphoreType.DMA((members,)),
            pltpu.SemaphoreType.DMA,
        ],
        compiler_params=pltpu.CompilerParams(collective_id=ident, has_side_effects=True),
    )(blocks)


def gelu_slope(value):
    return (
        0.5 * (1.0 + lax.erf(value * 0.7071067811865476))
        + value * jnp.exp(-0.5 * value * value) * 0.3989422804014327
    )


def local_pass(wave, lens, w_first, norm_gain, norm_bias, w_second, cot):
    rows, samp = wave.shape
    ker_first = w_first.shape[0]
    stride_first = ker_first // 2
    chans = w_first.shape[1]
    taps_second = w_second.shape[0]
    frames0 = (samp - ker_first) // stride_first + 1
    frames1 = (frames0 - taps_second) // 2 + 1
    blocks = wave[:, : stride_first * (frames0 + 1)].reshape(rows, frames0 + 1, stride_first)
    patches = jnp.concatenate([blocks[:, :-1], blocks[:, 1:]], axis=2).reshape(
        rows * frames0, ker_first
    )
    pre0 = jnp.dot(patches, w_first, preferred_element_type=jnp.float32).reshape(
        rows, frames0, chans
    )
    valid0 = (lens - ker_first) // stride_first + 1
    mask0 = (jnp.arange(frames0, dtype=jnp.int32)[None, :] < valid0[:, None]).astype(jnp.float32)[
        :, :, None
    ]
    count0 = valid0.astype(jnp.float32)[:, None, None]
    mean0 = jnp.sum(pre0 * mask0, axis=1, keepdims=True) / count0
    centred = (pre0 - mean0) * mask0
    var0 = jnp.sum(centred * centred, axis=1, keepdims=True) / count0
    inv_std = lax.rsqrt(var0 + 1e-05)
    normed = centred * inv_std
    lifted = normed * norm_gain + norm_bias
    act0 = (jax.nn.gelu(lifted, approximate=False) * mask0).astype(jnp.bfloat16)
    span = 2 * frames1
    taps = jnp.concatenate(
        [act0[:, 0:span:2], act0[:, 1:span:2], act0[:, 2 : span + 1 : 2]], axis=2
    )
    taps = taps.reshape(rows * frames1, taps_second * chans)
    kernel = w_second.reshape(taps_second * chans, chans)
    pre1 = jnp.dot(taps, kernel, preferred_element_type=jnp.float32).reshape(rows, frames1, chans)
    valid1 = (valid0 - taps_second) // 2 + 1
    mask1 = (jnp.arange(frames1, dtype=jnp.int32)[None, :] < valid1[:, None]).astype(jnp.float32)[
        :, :, None
    ]
    features = (jax.nn.gelu(pre1, approximate=False) * mask1).astype(jnp.bfloat16)
    grad1 = (
        (cot.astype(jnp.float32) * gelu_slope(pre1) * mask1)
        .astype(jnp.bfloat16)
        .reshape(rows * frames1, chans)
    )
    grad_kernel = lax.dot_general(
        grad1, taps, (((0,), (0,)), ((), ())), preferred_element_type=jnp.float32
    )
    back = lax.dot_general(
        grad1, kernel, (((1,), (1,)), ((), ())), preferred_element_type=jnp.float32
    )
    back = back.reshape(rows, frames1, taps_second, chans)
    zero_row = jnp.zeros((rows, 1, chans), jnp.float32)
    even = back[:, :, 0] + jnp.concatenate([zero_row, back[:, :-1, 2]], axis=1)
    odd = back[:, :, 1]
    pieces = [jnp.stack([even, odd], axis=2).reshape(rows, span, chans), back[:, -1:, 2]]
    dact0 = jnp.concatenate(pieces, axis=1)
    dlift = dact0 * gelu_slope(lifted) * mask0
    grad_gain = jnp.sum(dlift * normed, axis=(0, 1))
    grad_bias = jnp.sum(dlift, axis=(0, 1))
    dnorm = dlift * norm_gain
    first_mean = jnp.sum(dnorm, axis=1, keepdims=True) / count0
    second_mean = jnp.sum(dnorm * normed, axis=1, keepdims=True) / count0
    dpre0 = inv_std * (dnorm - first_mean - normed * second_mean) * mask0
    grad_filter = lax.dot_general(
        dpre0.reshape(rows * frames0, chans),
        patches.astype(jnp.float32),
        (((0,), (0,)), ((), ())),
        precision=lax.Precision.HIGHEST,
        preferred_element_type=jnp.float32,
    )
    small = jnp.concatenate([grad_filter, grad_gain[:, None], grad_bias[:, None]], axis=1)
    grads = (grad_kernel, small)
    return (features, grads)


def shards(wave, lengths, order, w_first, norm_gain, norm_bias, w_second, cot):
    members = lax.axis_size("dev")
    member = lax.axis_index("dev")
    rows = wave.shape[0]
    share = rows // members
    own_order = lax.dynamic_index_in_dim(order, member, 0, keepdims=False)
    dealt = own_order.reshape(share, members).T.reshape(rows)
    outgoing = jnp.take(wave, dealt, axis=0)
    arrived = lax.all_to_all(outgoing, "dev", split_axis=0, concat_axis=0, tiled=True)
    group_lens = jnp.take_along_axis(lengths.reshape(members, rows), order, axis=1)
    group_lens = group_lens.reshape(members, share, members)
    lens = lax.dynamic_index_in_dim(group_lens, member, 2, keepdims=False).reshape(rows)
    features, (grad_kernel, small) = local_pass(
        arrived, lens, w_first, norm_gain, norm_bias, w_second, cot
    )
    taps_second = w_second.shape[0]
    in_chans = w_second.shape[1]
    ker_first = w_first.shape[0]
    members = lax.axis_size("dev")
    groups = lax.axis_size("grp")
    full = jnp.concatenate([grad_kernel, small], axis=1)
    chans, span = full.shape
    width = chans // members
    halves = full.reshape(members, 2, width // 2, span)
    core = lax.rem(lax.axis_index("grp"), 2)
    keep = lax.dynamic_index_in_dim(halves, core, 1, keepdims=False)
    give = lax.dynamic_index_in_dim(halves, 1 - core, 1, keepdims=False)
    pairs = [(g, g ^ 1) for g in range(groups)]
    mine = keep + lax.ppermute(give, "grp", pairs)
    pieces = exchange(mine, members, "dev", False, 0)
    part = jnp.sum(pieces, axis=0)
    gathered = exchange(part[None], groups, "grp", True, 1)
    gathered = gathered.reshape(groups // 2, 2, width // 2, span)
    owned = jnp.sum(gathered, axis=0).reshape(width, span)
    grad_second = (
        owned[:, : taps_second * in_chans].reshape(width, taps_second, in_chans).transpose(1, 2, 0)
    )
    grad_first = owned[:, taps_second * in_chans : taps_second * in_chans + ker_first].T
    grad_gain = owned[:, taps_second * in_chans + ker_first]
    grad_bias = owned[:, taps_second * in_chans + ker_first + 1]
    return (features, grad_second, grad_first, grad_gain, grad_bias)


def solution(mesh):
    placed = (
        P(("grp", "dev"), None),
        P("grp"),
        P("grp", None),
        P(),
        P(),
        P(),
        P(),
        P(("grp", "dev"), None, None),
    )
    return jax.shard_map(
        shards,
        mesh=mesh,
        in_specs=placed,
        out_specs=(
            P(("grp", "dev"), None, None),
            P(None, None, "dev"),
            P(None, "dev"),
            P("dev"),
            P("dev"),
        ),
        check_vma=False,
    )
```

```python
import functools

import jax
import jax.numpy as jnp
from jax import lax
from jax.experimental import pallas as pl
from jax.experimental.pallas import tpu as pltpu
from jax.sharding import PartitionSpec as P

MESH = pl.DeviceIdType.MESH


def exchange_kernel(members, axis, stride, gather, src_ref, dst_ref, send_sems, recv_sems, local_sem):
    if axis == "grp":
        coord = lax.axis_index("grp")
        me = coord // stride
        offset = lax.rem(coord, stride)
        other = lax.axis_index("dev")
    else:
        me = lax.axis_index("dev")
        other = lax.axis_index("grp")

    def where(peer):
        return (peer * stride + offset, other) if axis == "grp" else (other, peer)

    def source(peer):
        return src_ref.at[0] if gather else src_ref.at[peer]

    barrier = pltpu.get_barrier_semaphore()

    def greet(step, carry):
        peer = lax.rem(me + step, members)
        pl.semaphore_signal(barrier, inc=1, device_id=where(peer), device_id_type=MESH)
        return carry

    lax.fori_loop(1, members, greet, 0)
    pl.semaphore_wait(barrier, members - 1)
    local = pltpu.make_async_copy(source(me), dst_ref.at[me], local_sem)
    local.start()

    def send(step, carry):
        peer = lax.rem(me + step, members)
        pltpu.make_async_remote_copy(
            src_ref=source(peer),
            dst_ref=dst_ref.at[me],
            send_sem=send_sems.at[step],
            recv_sem=recv_sems.at[step],
            device_id=where(peer),
            device_id_type=MESH,
        ).start()
        return carry

    lax.fori_loop(1, members, send, 0)

    def finish(step, carry):
        peer = lax.rem(me + step, members)
        sender = lax.rem(me + members - step, members)
        pltpu.make_async_remote_copy(
            src_ref=source(peer),
            dst_ref=dst_ref.at[me],
            send_sem=send_sems.at[step],
            recv_sem=recv_sems.at[step],
            device_id=where(peer),
            device_id_type=MESH,
        ).wait_send()
        pltpu.make_async_remote_copy(
            src_ref=source(me),
            dst_ref=dst_ref.at[sender],
            send_sem=send_sems.at[step],
            recv_sem=recv_sems.at[step],
            device_id=where(sender),
            device_id_type=MESH,
        ).wait_recv()
        return carry

    lax.fori_loop(1, members, finish, 0)
    local.wait()


def exchange(blocks, members, axis, stride, gather, ident):
    shape = (members,) + blocks.shape[1:]
    return pl.pallas_call(
        functools.partial(exchange_kernel, members, axis, stride, gather),
        out_shape=jax.ShapeDtypeStruct(shape, blocks.dtype),
        in_specs=[pl.BlockSpec(memory_space=pl.ANY)],
        out_specs=pl.BlockSpec(memory_space=pl.ANY),
        scratch_shapes=[
            pltpu.SemaphoreType.DMA((members,)),
            pltpu.SemaphoreType.DMA((members,)),
            pltpu.SemaphoreType.DMA,
        ],
        compiler_params=pltpu.CompilerParams(collective_id=ident, has_side_effects=True),
    )(blocks)


def gelu_slope(value):
    return (
        0.5 * (1.0 + lax.erf(value * 0.7071067811865476))
        + value * jnp.exp(-0.5 * value * value) * 0.3989422804014327
    )


def local_pass(wave, lens, w_first, norm_gain, norm_bias, w_second, cot):
    rows, samp = wave.shape
    ker_first = w_first.shape[0]
    stride_first = ker_first // 2
    chans = w_first.shape[1]
    taps_second = w_second.shape[0]
    frames0 = (samp - ker_first) // stride_first + 1
    frames1 = (frames0 - taps_second) // 2 + 1
    pairs = (frames0 + 1) // 2
    hop = 2 * stride_first
    reach = hop + stride_first
    padded = jnp.pad(wave, ((0, 0), (0, hop * (pairs + 1) - samp)))
    blocks = padded.reshape(rows, pairs + 1, hop)
    patches = jnp.concatenate([blocks[:, :-1], blocks[:, 1:, :stride_first]], axis=2)
    zeros_w = jnp.zeros((stride_first, chans), w_first.dtype)
    w_pair = jnp.concatenate(
        [
            jnp.concatenate([w_first, zeros_w], axis=0),
            jnp.concatenate([zeros_w, w_first], axis=0),
        ],
        axis=1,
    )
    pre0 = jnp.einsum("rum,mc->ruc", patches, w_pair, preferred_element_type=jnp.float32)
    valid0 = (lens - ker_first) // stride_first + 1
    frame = (
        2 * jnp.arange(pairs, dtype=jnp.int32)[:, None]
        + (jnp.arange(2 * chans, dtype=jnp.int32) // chans)[None, :]
    )
    mask0 = (frame[None] < valid0[:, None, None]).astype(jnp.float32)
    count0 = valid0.astype(jnp.float32)[:, None]

    def fold(x):
        s = jnp.sum(x, axis=1)
        return s[:, :chans] + s[:, chans:]

    def spread(x):
        return jnp.concatenate([x, x], axis=1)[:, None, :]

    mean0 = fold(pre0 * mask0) / count0
    centred = (pre0 - spread(mean0)) * mask0
    var0 = fold(centred * centred) / count0
    inv_std = spread(lax.rsqrt(var0 + 1e-05))
    normed = centred * inv_std
    gain2 = jnp.concatenate([norm_gain, norm_gain])
    bias2 = jnp.concatenate([norm_bias, norm_bias])
    lifted = normed * gain2 + bias2
    act0 = (jax.nn.gelu(lifted, approximate=False) * mask0).astype(jnp.bfloat16)
    taps = jnp.concatenate([act0[:, :frames1], act0[:, 1 : frames1 + 1, :chans]], axis=2)
    kernel = w_second.reshape(taps_second * chans, chans)
    pre1 = jnp.einsum("rui,io->ruo", taps, kernel, preferred_element_type=jnp.float32)
    valid1 = (valid0 - taps_second) // 2 + 1
    mask1 = (jnp.arange(frames1, dtype=jnp.int32)[None, :] < valid1[:, None]).astype(jnp.float32)[
        :, :, None
    ]
    features = (jax.nn.gelu(pre1, approximate=False) * mask1).astype(jnp.bfloat16)
    grad1 = (cot.astype(jnp.float32) * gelu_slope(pre1) * mask1).astype(jnp.bfloat16)
    grad_kernel = jnp.einsum("ruo,rui->oi", grad1, taps, preferred_element_type=jnp.float32)
    back = jnp.einsum("ruo,io->rui", grad1, kernel, preferred_element_type=jnp.float32)
    dact0 = jnp.pad(back[:, :, : 2 * chans], ((0, 0), (0, pairs - frames1), (0, 0))) + jnp.pad(
        back[:, :, 2 * chans :], ((0, 0), (1, pairs - frames1 - 1), (0, chans))
    )
    dlift = dact0 * gelu_slope(lifted) * mask0
    gain_terms = jnp.sum(dlift * normed, axis=(0, 1))
    bias_terms = jnp.sum(dlift, axis=(0, 1))
    grad_gain = gain_terms[:chans] + gain_terms[chans:]
    grad_bias = bias_terms[:chans] + bias_terms[chans:]
    dnorm = dlift * gain2
    first_mean = spread(fold(dnorm) / count0)
    second_mean = spread(fold(dnorm * normed) / count0)
    dpre0 = inv_std * (dnorm - first_mean - normed * second_mean) * mask0
    grad_pair = jnp.einsum(
        "ruj,rum->jm",
        dpre0,
        patches.astype(jnp.float32),
        precision=lax.Precision.HIGHEST,
        preferred_element_type=jnp.float32,
    )
    grad_filter = grad_pair[:chans, :ker_first] + grad_pair[chans:, stride_first:]
    small = jnp.concatenate([grad_filter, grad_gain[:, None], grad_bias[:, None]], axis=1)
    grads = (grad_kernel, small)
    return (features, grads)


def shards(wave, lengths, order, w_first, norm_gain, norm_bias, w_second, cot):
    members = lax.axis_size("dev")
    member = lax.axis_index("dev")
    rows = wave.shape[0]
    share = rows // members
    own_order = lax.dynamic_index_in_dim(order, member, 0, keepdims=False)
    dealt = own_order.reshape(share, members).T.reshape(rows)
    outgoing = jnp.take(wave, dealt, axis=0)
    arrived = lax.all_to_all(outgoing, "dev", split_axis=0, concat_axis=0, tiled=True)
    group_lens = jnp.take_along_axis(lengths.reshape(members, rows), order, axis=1)
    group_lens = group_lens.reshape(members, share, members)
    lens = lax.dynamic_index_in_dim(group_lens, member, 2, keepdims=False).reshape(rows)
    features, (grad_kernel, small) = local_pass(
        arrived, lens, w_first, norm_gain, norm_bias, w_second, cot
    )
    taps_second = w_second.shape[0]
    in_chans = w_second.shape[1]
    ker_first = w_first.shape[0]
    members = lax.axis_size("dev")
    groups = lax.axis_size("grp")
    full = jnp.concatenate([grad_kernel, small], axis=1)
    chans, span = full.shape
    width = chans // members
    halves = full.reshape(members, 2, width // 2, span)
    core = lax.rem(lax.axis_index("grp"), 2)
    keep = lax.dynamic_index_in_dim(halves, core, 1, keepdims=False)
    give = lax.dynamic_index_in_dim(halves, 1 - core, 1, keepdims=False)
    pairs = [(g, g ^ 1) for g in range(groups)]
    mine = keep + lax.ppermute(give, "grp", pairs)
    pieces = exchange(mine, members, "dev", 1, False, 0)
    part = jnp.sum(pieces, axis=0)
    rows_y = groups // 2
    scattered = exchange(part.reshape(rows_y, (width // 2) // rows_y, span), rows_y, "grp", 2, False, 1)
    total = jnp.sum(scattered, axis=0)
    gathered = exchange(total[None], groups, "grp", 1, True, 2)
    gathered = gathered.reshape(rows_y, 2, (width // 2) // rows_y, span)
    owned = gathered.transpose(1, 0, 2, 3).reshape(width, span)
    grad_second = (
        owned[:, : taps_second * in_chans].reshape(width, taps_second, in_chans).transpose(1, 2, 0)
    )
    grad_first = owned[:, taps_second * in_chans : taps_second * in_chans + ker_first].T
    grad_gain = owned[:, taps_second * in_chans + ker_first]
    grad_bias = owned[:, taps_second * in_chans + ker_first + 1]
    return (features, grad_second, grad_first, grad_gain, grad_bias)


def solution(mesh):
    placed = (
        P(("grp", "dev"), None),
        P("grp"),
        P("grp", None),
        P(),
        P(),
        P(),
        P(),
        P(("grp", "dev"), None, None),
    )
    return jax.shard_map(
        shards,
        mesh=mesh,
        in_specs=placed,
        out_specs=(
            P(("grp", "dev"), None, None),
            P(None, None, "dev"),
            P(None, "dev"),
            P("dev"),
            P("dev"),
        ),
        check_vma=False,
    )
```

```python
import functools

import jax
import jax.numpy as jnp
from jax import lax
from jax.experimental import pallas as pl
from jax.experimental.pallas import tpu as pltpu
from jax.sharding import PartitionSpec as P

MESH = pl.DeviceIdType.MESH


def exchange_kernel(members, axis, stride, gather, count, *refs):
    srcs = refs[:count]
    dsts = refs[count : 2 * count]
    send_sems, recv_sems, local_sems = refs[2 * count :]
    if axis == "grp":
        coord = lax.axis_index("grp")
        me = coord // stride
        offset = lax.rem(coord, stride)
        other = lax.axis_index("dev")
    else:
        me = lax.axis_index("dev")
        other = lax.axis_index("grp")

    def where(peer):
        return (peer * stride + offset, other) if axis == "grp" else (other, peer)

    def source(a, peer):
        return srcs[a].at[0] if gather else srcs[a].at[peer]

    def remote(a, step, peer, src_peer, slot):
        return pltpu.make_async_remote_copy(
            src_ref=source(a, src_peer),
            dst_ref=dsts[a].at[slot],
            send_sem=send_sems.at[a, step],
            recv_sem=recv_sems.at[a, step],
            device_id=where(peer),
            device_id_type=MESH,
        )

    barrier = pltpu.get_barrier_semaphore()

    def greet(step, carry):
        peer = lax.rem(me + step, members)
        pl.semaphore_signal(barrier, inc=1, device_id=where(peer), device_id_type=MESH)
        return carry

    lax.fori_loop(1, members, greet, 0)
    pl.semaphore_wait(barrier, members - 1)
    locals_ = [
        pltpu.make_async_copy(source(a, me), dsts[a].at[me], local_sems.at[a]) for a in range(count)
    ]
    for local in locals_:
        local.start()

    def send(step, carry):
        peer = lax.rem(me + step, members)
        for a in range(count):
            remote(a, step, peer, peer, me).start()
        return carry

    lax.fori_loop(1, members, send, 0)

    def finish(step, carry):
        peer = lax.rem(me + step, members)
        sender = lax.rem(me + members - step, members)
        for a in range(count):
            remote(a, step, peer, peer, me).wait_send()
            remote(a, step, sender, me, sender).wait_recv()
        return carry

    lax.fori_loop(1, members, finish, 0)
    for local in locals_:
        local.wait()


def exchange(blocks, members, axis, stride, gather, ident):
    count = len(blocks)
    shapes = [jax.ShapeDtypeStruct((members,) + b.shape[1:], b.dtype) for b in blocks]
    return pl.pallas_call(
        functools.partial(exchange_kernel, members, axis, stride, gather, count),
        out_shape=shapes,
        in_specs=[pl.BlockSpec(memory_space=pl.ANY)] * count,
        out_specs=[pl.BlockSpec(memory_space=pl.ANY)] * count,
        scratch_shapes=[
            pltpu.SemaphoreType.DMA((count, members)),
            pltpu.SemaphoreType.DMA((count, members)),
            pltpu.SemaphoreType.DMA((count,)),
        ],
        compiler_params=pltpu.CompilerParams(collective_id=ident, has_side_effects=True),
    )(*blocks)


def gelu_slope(value):
    return (
        0.5 * (1.0 + lax.erf(value * 0.7071067811865476))
        + value * jnp.exp(-0.5 * value * value) * 0.3989422804014327
    )


def local_pass(wave, lens, w_first, norm_gain, norm_bias, w_second, cot):
    rows, samp = wave.shape
    ker_first = w_first.shape[0]
    stride_first = ker_first // 2
    chans = w_first.shape[1]
    taps_second = w_second.shape[0]
    frames0 = (samp - ker_first) // stride_first + 1
    frames1 = (frames0 - taps_second) // 2 + 1
    pairs = (frames0 + 1) // 2
    hop = 2 * stride_first
    reach = hop + stride_first
    padded = jnp.pad(wave, ((0, 0), (0, hop * (pairs + 1) - samp)))
    blocks = padded.reshape(rows, pairs + 1, hop)
    patches = jnp.concatenate([blocks[:, :-1], blocks[:, 1:, :stride_first]], axis=2)
    zeros_w = jnp.zeros((stride_first, chans), w_first.dtype)
    w_pair = jnp.concatenate(
        [
            jnp.concatenate([w_first, zeros_w], axis=0),
            jnp.concatenate([zeros_w, w_first], axis=0),
        ],
        axis=1,
    )
    pre0 = jnp.einsum("rum,mc->ruc", patches, w_pair, preferred_element_type=jnp.float32)
    valid0 = (lens - ker_first) // stride_first + 1
    frame = (
        2 * jnp.arange(pairs, dtype=jnp.int32)[:, None]
        + (jnp.arange(2 * chans, dtype=jnp.int32) // chans)[None, :]
    )
    mask0 = (frame[None] < valid0[:, None, None]).astype(jnp.float32)
    count0 = valid0.astype(jnp.float32)[:, None]

    def fold(x):
        s = jnp.sum(x, axis=1)
        return s[:, :chans] + s[:, chans:]

    def spread(x):
        return jnp.concatenate([x, x], axis=1)[:, None, :]

    mean0 = fold(pre0 * mask0) / count0
    centred = (pre0 - spread(mean0)) * mask0
    var0 = fold(centred * centred) / count0
    inv_std = spread(lax.rsqrt(var0 + 1e-05))
    normed = centred * inv_std
    gain2 = jnp.concatenate([norm_gain, norm_gain])
    bias2 = jnp.concatenate([norm_bias, norm_bias])
    lifted = normed * gain2 + bias2
    act0 = (jax.nn.gelu(lifted, approximate=False) * mask0).astype(jnp.bfloat16)
    taps = jnp.concatenate([act0[:, :frames1], act0[:, 1 : frames1 + 1, :chans]], axis=2)
    kernel = w_second.reshape(taps_second * chans, chans)
    pre1 = jnp.einsum("rui,io->ruo", taps, kernel, preferred_element_type=jnp.float32)
    valid1 = (valid0 - taps_second) // 2 + 1
    mask1 = (jnp.arange(frames1, dtype=jnp.int32)[None, :] < valid1[:, None]).astype(jnp.float32)[
        :, :, None
    ]
    features = (jax.nn.gelu(pre1, approximate=False) * mask1).astype(jnp.bfloat16)
    grad1 = (cot.astype(jnp.float32) * gelu_slope(pre1) * mask1).astype(jnp.bfloat16)
    members = lax.axis_size("dev")
    width = chans // members
    split = grad1.reshape(rows, frames1, members, 2, width // 2)
    grad_kernel = jnp.einsum(
        "rudhj,rui->hdji", split, taps, preferred_element_type=jnp.float32
    )
    back = jnp.einsum("ruo,io->rui", grad1, kernel, preferred_element_type=jnp.float32)
    dact0 = jnp.pad(back[:, :, : 2 * chans], ((0, 0), (0, pairs - frames1), (0, 0))) + jnp.pad(
        back[:, :, 2 * chans :], ((0, 0), (1, pairs - frames1 - 1), (0, chans))
    )
    dlift = dact0 * gelu_slope(lifted) * mask0
    gain_terms = jnp.sum(dlift * normed, axis=(0, 1))
    bias_terms = jnp.sum(dlift, axis=(0, 1))
    grad_gain = gain_terms[:chans] + gain_terms[chans:]
    grad_bias = bias_terms[:chans] + bias_terms[chans:]
    dnorm = dlift * gain2
    first_mean = spread(fold(dnorm) / count0)
    second_mean = spread(fold(dnorm * normed) / count0)
    dpre0 = inv_std * (dnorm - first_mean - normed * second_mean) * mask0
    grad_pair = jnp.einsum(
        "ruj,rum->jm",
        dpre0,
        patches.astype(jnp.float32),
        precision=lax.Precision.HIGHEST,
        preferred_element_type=jnp.float32,
    )
    grad_filter = grad_pair[:chans, :ker_first] + grad_pair[chans:, stride_first:]
    small = jnp.concatenate([grad_filter, grad_gain[:, None], grad_bias[:, None]], axis=1)
    small = small.reshape(members, 2, width // 2, small.shape[1]).transpose(1, 0, 2, 3)
    grads = (grad_kernel, small)
    return (features, grads)


def shards(wave, lengths, order, w_first, norm_gain, norm_bias, w_second, cot):
    members = lax.axis_size("dev")
    member = lax.axis_index("dev")
    rows = wave.shape[0]
    share = rows // members
    own_order = lax.dynamic_index_in_dim(order, member, 0, keepdims=False)
    dealt = own_order.reshape(share, members).T.reshape(rows)
    outgoing = jnp.take(wave, dealt, axis=0)
    arrived = lax.all_to_all(outgoing, "dev", split_axis=0, concat_axis=0, tiled=True)
    picks = lax.dynamic_index_in_dim(
        order.reshape(members, share, members), member, 2, keepdims=False
    )
    slots = jnp.arange(rows, dtype=jnp.int32)
    hits = picks[:, :, None] == slots[None, None, :]
    lens = jnp.sum(
        jnp.where(hits, lengths.reshape(members, 1, rows), 0), axis=2, dtype=jnp.int32
    ).reshape(rows)
    features, (grad_kernel, small) = local_pass(
        arrived, lens, w_first, norm_gain, norm_bias, w_second, cot
    )
    taps_second = w_second.shape[0]
    in_chans = w_second.shape[1]
    ker_first = w_first.shape[0]
    members = lax.axis_size("dev")
    groups = lax.axis_size("grp")
    core = lax.rem(lax.axis_index("grp"), 2)
    pairs = [(g, g ^ 1) for g in range(groups)]

    def pair_sum(halves):
        keep = lax.dynamic_index_in_dim(halves, core, 0, keepdims=False)
        give = lax.dynamic_index_in_dim(halves, 1 - core, 0, keepdims=False)
        return keep + lax.ppermute(give, "grp", pairs)

    mine_kernel = pair_sum(grad_kernel).astype(jnp.bfloat16)
    mine_small = pair_sum(small)
    pieces_kernel, pieces_small = exchange(
        [mine_kernel, mine_small], members, "dev", 1, False, 0
    )
    part = jnp.concatenate(
        [jnp.sum(pieces_kernel.astype(jnp.float32), axis=0), jnp.sum(pieces_small, axis=0)],
        axis=1,
    )
    chans = w_second.shape[2]
    width = chans // members
    span = part.shape[1]
    rows_y = groups // 2
    (scattered,) = exchange(
        [part.reshape(rows_y, (width // 2) // rows_y, span)], rows_y, "grp", 2, False, 1
    )
    total = jnp.sum(scattered, axis=0)
    (gathered,) = exchange([total[None]], groups, "grp", 1, True, 2)
    gathered = gathered.reshape(rows_y, 2, (width // 2) // rows_y, span)
    owned = gathered.transpose(1, 0, 2, 3).reshape(width, span)
    grad_second = (
        owned[:, : taps_second * in_chans].reshape(width, taps_second, in_chans).transpose(1, 2, 0)
    )
    grad_first = owned[:, taps_second * in_chans : taps_second * in_chans + ker_first].T
    grad_gain = owned[:, taps_second * in_chans + ker_first]
    grad_bias = owned[:, taps_second * in_chans + ker_first + 1]
    return (features, grad_second, grad_first, grad_gain, grad_bias)


def solution(mesh):
    placed = (
        P(("grp", "dev"), None),
        P("grp"),
        P("grp", None),
        P(),
        P(),
        P(),
        P(),
        P(("grp", "dev"), None, None),
    )
    return jax.shard_map(
        shards,
        mesh=mesh,
        in_specs=placed,
        out_specs=(
            P(("grp", "dev"), None, None),
            P(None, None, "dev"),
            P(None, "dev"),
            P("dev"),
            P("dev"),
        ),
        check_vma=False,
    )
```

```python
import functools

import jax
import jax.numpy as jnp
from jax import lax
from jax.experimental import pallas as pl
from jax.experimental.pallas import tpu as pltpu
from jax.sharding import PartitionSpec as P

MESH = pl.DeviceIdType.MESH


def exchange_kernel(members, axis, stride, gather, count, *refs):
    srcs = refs[:count]
    dsts = refs[count : 2 * count]
    send_sems, recv_sems, local_sems = refs[2 * count :]
    if axis == "grp":
        coord = lax.axis_index("grp")
        me = coord // stride
        offset = lax.rem(coord, stride)
        other = lax.axis_index("dev")
    else:
        me = lax.axis_index("dev")
        other = lax.axis_index("grp")

    def where(peer):
        return (peer * stride + offset, other) if axis == "grp" else (other, peer)

    def source(a, peer):
        return srcs[a].at[0] if gather else srcs[a].at[peer]

    def remote(a, step, peer, src_peer, slot):
        return pltpu.make_async_remote_copy(
            src_ref=source(a, src_peer),
            dst_ref=dsts[a].at[slot],
            send_sem=send_sems.at[a, step],
            recv_sem=recv_sems.at[a, step],
            device_id=where(peer),
            device_id_type=MESH,
        )

    barrier = pltpu.get_barrier_semaphore()

    def greet(step, carry):
        peer = lax.rem(me + step, members)
        pl.semaphore_signal(barrier, inc=1, device_id=where(peer), device_id_type=MESH)
        return carry

    lax.fori_loop(1, members, greet, 0)
    pl.semaphore_wait(barrier, members - 1)
    locals_ = [
        pltpu.make_async_copy(source(a, me), dsts[a].at[me], local_sems.at[a]) for a in range(count)
    ]
    for local in locals_:
        local.start()

    def send(step, carry):
        peer = lax.rem(me + step, members)
        for a in range(count):
            remote(a, step, peer, peer, me).start()
        return carry

    lax.fori_loop(1, members, send, 0)

    def finish(step, carry):
        peer = lax.rem(me + step, members)
        sender = lax.rem(me + members - step, members)
        for a in range(count):
            remote(a, step, peer, peer, me).wait_send()
            remote(a, step, sender, me, sender).wait_recv()
        return carry

    lax.fori_loop(1, members, finish, 0)
    for local in locals_:
        local.wait()


def exchange(blocks, members, axis, stride, gather, ident):
    count = len(blocks)
    shapes = [jax.ShapeDtypeStruct((members,) + b.shape[1:], b.dtype) for b in blocks]
    return pl.pallas_call(
        functools.partial(exchange_kernel, members, axis, stride, gather, count),
        out_shape=shapes,
        in_specs=[pl.BlockSpec(memory_space=pl.ANY)] * count,
        out_specs=[pl.BlockSpec(memory_space=pl.ANY)] * count,
        scratch_shapes=[
            pltpu.SemaphoreType.DMA((count, members)),
            pltpu.SemaphoreType.DMA((count, members)),
            pltpu.SemaphoreType.DMA((count,)),
        ],
        compiler_params=pltpu.CompilerParams(collective_id=ident, has_side_effects=True),
    )(*blocks)


def gelu_slope(value):
    return (
        0.5 * (1.0 + lax.erf(value * 0.7071067811865476))
        + value * jnp.exp(-0.5 * value * value) * 0.3989422804014327
    )


def local_pass(wave, lens, w_first, norm_gain, norm_bias, w_second, cot):
    rows, samp = wave.shape
    ker_first = w_first.shape[0]
    stride_first = ker_first // 2
    chans = w_first.shape[1]
    taps_second = w_second.shape[0]
    frames0 = (samp - ker_first) // stride_first + 1
    frames1 = (frames0 - taps_second) // 2 + 1
    pairs = (frames0 + 1) // 2
    hop = 2 * stride_first
    reach = hop + stride_first
    padded = jnp.pad(wave, ((0, 0), (0, hop * (pairs + 1) - samp)))
    blocks = padded.reshape(rows, pairs + 1, hop)
    patches = jnp.concatenate([blocks[:, :-1], blocks[:, 1:, :stride_first]], axis=2)
    zeros_w = jnp.zeros((stride_first, chans), w_first.dtype)
    w_pair = jnp.concatenate(
        [
            jnp.concatenate([w_first, zeros_w], axis=0),
            jnp.concatenate([zeros_w, w_first], axis=0),
        ],
        axis=1,
    )
    pre0 = jnp.einsum("rum,mc->ruc", patches, w_pair, preferred_element_type=jnp.float32)
    valid0 = (lens - ker_first) // stride_first + 1
    frame = (
        2 * jnp.arange(pairs, dtype=jnp.int32)[:, None]
        + (jnp.arange(2 * chans, dtype=jnp.int32) // chans)[None, :]
    )
    mask0 = (frame[None] < valid0[:, None, None]).astype(jnp.float32)
    count0 = valid0.astype(jnp.float32)[:, None]

    def fold(x):
        s = jnp.sum(x, axis=1)
        return s[:, :chans] + s[:, chans:]

    def spread(x):
        return jnp.concatenate([x, x], axis=1)[:, None, :]

    mean0 = fold(pre0 * mask0) / count0
    centred = (pre0 - spread(mean0)) * mask0
    var0 = fold(centred * centred) / count0
    inv_std = spread(lax.rsqrt(var0 + 1e-05))
    normed = centred * inv_std
    gain2 = jnp.concatenate([norm_gain, norm_gain])
    bias2 = jnp.concatenate([norm_bias, norm_bias])
    lifted = normed * gain2 + bias2
    act0 = (jax.nn.gelu(lifted, approximate=False) * mask0).astype(jnp.bfloat16)
    taps = jnp.concatenate([act0[:, :frames1], act0[:, 1 : frames1 + 1, :chans]], axis=2)
    kernel = w_second.reshape(taps_second * chans, chans)
    pre1 = jnp.einsum("rui,io->ruo", taps, kernel, preferred_element_type=jnp.float32)
    valid1 = (valid0 - taps_second) // 2 + 1
    mask1 = (jnp.arange(frames1, dtype=jnp.int32)[None, :] < valid1[:, None]).astype(jnp.float32)[
        :, :, None
    ]
    features = (jax.nn.gelu(pre1, approximate=False) * mask1).astype(jnp.bfloat16)
    grad1 = (cot.astype(jnp.float32) * gelu_slope(pre1) * mask1).astype(jnp.bfloat16)
    members = lax.axis_size("dev")
    width = chans // members
    grad_kernel = jnp.einsum("ruo,rui->oi", grad1, taps, preferred_element_type=jnp.float32)
    grad_kernel = grad_kernel.reshape(members, 2, width // 2, -1).transpose(1, 0, 2, 3)
    back = jnp.einsum("ruo,io->rui", grad1, kernel, preferred_element_type=jnp.float32)
    dact0 = jnp.pad(back[:, :, : 2 * chans], ((0, 0), (0, pairs - frames1), (0, 0))) + jnp.pad(
        back[:, :, 2 * chans :], ((0, 0), (1, pairs - frames1 - 1), (0, chans))
    )
    dlift = dact0 * gelu_slope(lifted) * mask0
    gain_terms = jnp.sum(dlift * normed, axis=(0, 1))
    bias_terms = jnp.sum(dlift, axis=(0, 1))
    grad_gain = gain_terms[:chans] + gain_terms[chans:]
    grad_bias = bias_terms[:chans] + bias_terms[chans:]
    dnorm = dlift * gain2
    first_mean = spread(fold(dnorm) / count0)
    second_mean = spread(fold(dnorm * normed) / count0)
    dpre0 = inv_std * (dnorm - first_mean - normed * second_mean) * mask0
    high = dpre0.astype(jnp.bfloat16)
    low = (dpre0 - high.astype(jnp.float32)).astype(jnp.bfloat16)
    grad_pair = jnp.einsum(
        "ruj,rum->jm", high, patches, preferred_element_type=jnp.float32
    ) + jnp.einsum("ruj,rum->jm", low, patches, preferred_element_type=jnp.float32)
    grad_filter = grad_pair[:chans, :ker_first] + grad_pair[chans:, stride_first:]
    small = jnp.concatenate([grad_filter, grad_gain[:, None], grad_bias[:, None]], axis=1)
    small = small.reshape(members, 2, width // 2, small.shape[1]).transpose(1, 0, 2, 3)
    grads = (grad_kernel, small)
    return (features, grads)


def shards(wave, lengths, order, w_first, norm_gain, norm_bias, w_second, cot):
    members = lax.axis_size("dev")
    member = lax.axis_index("dev")
    rows = wave.shape[0]
    share = rows // members
    own_order = lax.dynamic_index_in_dim(order, member, 0, keepdims=False)
    dealt = own_order.reshape(share, members).T.reshape(rows)
    outgoing = jnp.take(wave, dealt, axis=0)
    arrived = lax.all_to_all(outgoing, "dev", split_axis=0, concat_axis=0, tiled=True)
    picks = lax.dynamic_index_in_dim(
        order.reshape(members, share, members), member, 2, keepdims=False
    )
    slots = jnp.arange(rows, dtype=jnp.int32)
    hits = picks[:, :, None] == slots[None, None, :]
    lens = jnp.sum(
        jnp.where(hits, lengths.reshape(members, 1, rows), 0), axis=2, dtype=jnp.int32
    ).reshape(rows)
    features, (grad_kernel, small) = local_pass(
        arrived, lens, w_first, norm_gain, norm_bias, w_second, cot
    )
    taps_second = w_second.shape[0]
    in_chans = w_second.shape[1]
    ker_first = w_first.shape[0]
    members = lax.axis_size("dev")
    groups = lax.axis_size("grp")
    core = lax.rem(lax.axis_index("grp"), 2)
    pairs = [(g, g ^ 1) for g in range(groups)]

    def pair_sum(halves):
        keep = lax.dynamic_index_in_dim(halves, core, 0, keepdims=False)
        give = lax.dynamic_index_in_dim(halves, 1 - core, 0, keepdims=False)
        return keep + lax.ppermute(give, "grp", pairs)

    mine_kernel = pair_sum(grad_kernel).astype(jnp.bfloat16)
    mine_small = pair_sum(small)
    pieces_kernel, pieces_small = exchange(
        [mine_kernel, mine_small], members, "dev", 1, False, 0
    )
    part = jnp.concatenate(
        [jnp.sum(pieces_kernel.astype(jnp.float32), axis=0), jnp.sum(pieces_small, axis=0)],
        axis=1,
    )
    chans = w_second.shape[2]
    width = chans // members
    span = part.shape[1]
    rows_y = groups // 2
    (scattered,) = exchange(
        [part.reshape(rows_y, (width // 2) // rows_y, span)], rows_y, "grp", 2, False, 1
    )
    total = jnp.sum(scattered, axis=0)
    (gathered,) = exchange([total[None]], groups, "grp", 1, True, 2)
    gathered = gathered.reshape(rows_y, 2, (width // 2) // rows_y, span)
    owned = gathered.transpose(1, 0, 2, 3).reshape(width, span)
    grad_second = (
        owned[:, : taps_second * in_chans].reshape(width, taps_second, in_chans).transpose(1, 2, 0)
    )
    grad_first = owned[:, taps_second * in_chans : taps_second * in_chans + ker_first].T
    grad_gain = owned[:, taps_second * in_chans + ker_first]
    grad_bias = owned[:, taps_second * in_chans + ker_first + 1]
    return (features, grad_second, grad_first, grad_gain, grad_bias)


def solution(mesh):
    placed = (
        P(("grp", "dev"), None),
        P("grp"),
        P("grp", None),
        P(),
        P(),
        P(),
        P(),
        P(("grp", "dev"), None, None),
    )
    return jax.shard_map(
        shards,
        mesh=mesh,
        in_specs=placed,
        out_specs=(
            P(("grp", "dev"), None, None),
            P(None, None, "dev"),
            P(None, "dev"),
            P("dev"),
            P("dev"),
        ),
        check_vma=False,
    )
```

```python
import functools

import jax
import jax.numpy as jnp
from jax import lax
from jax.experimental import pallas as pl
from jax.experimental.pallas import tpu as pltpu
from jax.sharding import PartitionSpec as P

MESH = pl.DeviceIdType.MESH


def exchange_kernel(members, axis, stride, gather, count, *refs):
    srcs = refs[:count]
    dsts = refs[count : 2 * count]
    send_sems, recv_sems, local_sems = refs[2 * count :]
    if axis == "grp":
        coord = lax.axis_index("grp")
        me = coord // stride
        offset = lax.rem(coord, stride)
        other = lax.axis_index("dev")
    else:
        me = lax.axis_index("dev")
        other = lax.axis_index("grp")

    def where(peer):
        return (peer * stride + offset, other) if axis == "grp" else (other, peer)

    def source(a, peer):
        return srcs[a].at[0] if gather else srcs[a].at[peer]

    def remote(a, step, peer, src_peer, slot):
        return pltpu.make_async_remote_copy(
            src_ref=source(a, src_peer),
            dst_ref=dsts[a].at[slot],
            send_sem=send_sems.at[a, step],
            recv_sem=recv_sems.at[a, step],
            device_id=where(peer),
            device_id_type=MESH,
        )

    barrier = pltpu.get_barrier_semaphore()

    def greet(step, carry):
        peer = lax.rem(me + step, members)
        pl.semaphore_signal(barrier, inc=1, device_id=where(peer), device_id_type=MESH)
        return carry

    lax.fori_loop(1, members, greet, 0)
    pl.semaphore_wait(barrier, members - 1)
    locals_ = [
        pltpu.make_async_copy(source(a, me), dsts[a].at[me], local_sems.at[a]) for a in range(count)
    ]
    for local in locals_:
        local.start()

    def send(step, carry):
        peer = lax.rem(me + step, members)
        for a in range(count):
            remote(a, step, peer, peer, me).start()
        return carry

    lax.fori_loop(1, members, send, 0)

    def finish(step, carry):
        peer = lax.rem(me + step, members)
        sender = lax.rem(me + members - step, members)
        for a in range(count):
            remote(a, step, peer, peer, me).wait_send()
            remote(a, step, sender, me, sender).wait_recv()
        return carry

    lax.fori_loop(1, members, finish, 0)
    for local in locals_:
        local.wait()


def exchange(blocks, members, axis, stride, gather, ident):
    count = len(blocks)
    shapes = [jax.ShapeDtypeStruct((members,) + b.shape[1:], b.dtype) for b in blocks]
    return pl.pallas_call(
        functools.partial(exchange_kernel, members, axis, stride, gather, count),
        out_shape=shapes,
        in_specs=[pl.BlockSpec(memory_space=pl.ANY)] * count,
        out_specs=[pl.BlockSpec(memory_space=pl.ANY)] * count,
        scratch_shapes=[
            pltpu.SemaphoreType.DMA((count, members)),
            pltpu.SemaphoreType.DMA((count, members)),
            pltpu.SemaphoreType.DMA((count,)),
        ],
        compiler_params=pltpu.CompilerParams(collective_id=ident, has_side_effects=True),
    )(*blocks)


def reduce_gather_kernel(rows_y, src_ref, out_ref, stage, total, sends, recvs, shares, gets, local_sems):
    coord = lax.axis_index("grp")
    other = lax.axis_index("dev")
    groups = 2 * rows_y
    me = coord // 2
    core = lax.rem(coord, 2)
    barrier = pltpu.get_barrier_semaphore()

    def greet(step, carry):
        peer = lax.rem(coord + step, groups)
        pl.semaphore_signal(barrier, inc=1, device_id=(peer, other), device_id_type=MESH)
        return carry

    lax.fori_loop(1, groups, greet, 0)
    pl.semaphore_wait(barrier, groups - 1)
    own = pltpu.make_async_copy(src_ref.at[me], stage.at[me], local_sems.at[0])
    own.start()

    def scatter(step, peer, src_peer, slot):
        return pltpu.make_async_remote_copy(
            src_ref=src_ref.at[src_peer],
            dst_ref=stage.at[slot],
            send_sem=sends.at[step],
            recv_sem=recvs.at[step],
            device_id=(peer * 2 + core, other),
            device_id_type=MESH,
        )

    def send_part(step, carry):
        peer = lax.rem(me + step, rows_y)
        scatter(step, peer, peer, me).start()
        return carry

    lax.fori_loop(1, rows_y, send_part, 0)

    def finish_part(step, carry):
        peer = lax.rem(me + step, rows_y)
        sender = lax.rem(me + rows_y - step, rows_y)
        scatter(step, peer, peer, me).wait_send()
        scatter(step, sender, me, sender).wait_recv()
        return carry

    lax.fori_loop(1, rows_y, finish_part, 0)
    own.wait()
    total[...] = jnp.sum(stage[...], axis=0)
    mine = pltpu.make_async_copy(total, out_ref.at[coord], local_sems.at[1])
    mine.start()

    def spread(step, peer, slot):
        return pltpu.make_async_remote_copy(
            src_ref=total,
            dst_ref=out_ref.at[slot],
            send_sem=shares.at[step],
            recv_sem=gets.at[step],
            device_id=(peer, other),
            device_id_type=MESH,
        )

    def send_total(step, carry):
        spread(step, lax.rem(coord + step, groups), coord).start()
        return carry

    lax.fori_loop(1, groups, send_total, 0)

    def finish_total(step, carry):
        spread(step, lax.rem(coord + step, groups), coord).wait_send()
        sender = lax.rem(coord + groups - step, groups)
        spread(step, sender, sender).wait_recv()
        return carry

    lax.fori_loop(1, groups, finish_total, 0)
    mine.wait()


def reduce_gather(part, ident):
    rows_y, depth, span = part.shape
    groups = 2 * rows_y
    return pl.pallas_call(
        functools.partial(reduce_gather_kernel, rows_y),
        out_shape=jax.ShapeDtypeStruct((groups, depth, span), part.dtype),
        in_specs=[pl.BlockSpec(memory_space=pl.ANY)],
        out_specs=pl.BlockSpec(memory_space=pl.ANY),
        scratch_shapes=[
            pltpu.VMEM((rows_y, depth, span), part.dtype),
            pltpu.VMEM((depth, span), part.dtype),
            pltpu.SemaphoreType.DMA((rows_y,)),
            pltpu.SemaphoreType.DMA((rows_y,)),
            pltpu.SemaphoreType.DMA((groups,)),
            pltpu.SemaphoreType.DMA((groups,)),
            pltpu.SemaphoreType.DMA((2,)),
        ],
        compiler_params=pltpu.CompilerParams(collective_id=ident, has_side_effects=True),
    )(part)


def gelu_slope(value):
    return (
        0.5 * (1.0 + lax.erf(value * 0.7071067811865476))
        + value * jnp.exp(-0.5 * value * value) * 0.3989422804014327
    )


def local_pass(wave, lens, w_first, norm_gain, norm_bias, w_second, cot):
    rows, samp = wave.shape
    ker_first = w_first.shape[0]
    stride_first = ker_first // 2
    chans = w_first.shape[1]
    taps_second = w_second.shape[0]
    frames0 = (samp - ker_first) // stride_first + 1
    frames1 = (frames0 - taps_second) // 2 + 1
    pairs = (frames0 + 1) // 2
    hop = 2 * stride_first
    reach = hop + stride_first
    padded = jnp.pad(wave, ((0, 0), (0, hop * (pairs + 1) - samp)))
    blocks = padded.reshape(rows, pairs + 1, hop)
    patches = jnp.concatenate([blocks[:, :-1], blocks[:, 1:, :stride_first]], axis=2)
    zeros_w = jnp.zeros((stride_first, chans), w_first.dtype)
    w_pair = jnp.concatenate(
        [
            jnp.concatenate([w_first, zeros_w], axis=0),
            jnp.concatenate([zeros_w, w_first], axis=0),
        ],
        axis=1,
    )
    pre0 = jnp.einsum("rum,mc->ruc", patches, w_pair, preferred_element_type=jnp.float32)
    valid0 = (lens - ker_first) // stride_first + 1
    frame = (
        2 * jnp.arange(pairs, dtype=jnp.int32)[:, None]
        + (jnp.arange(2 * chans, dtype=jnp.int32) // chans)[None, :]
    )
    mask0 = (frame[None] < valid0[:, None, None]).astype(jnp.float32)
    count0 = valid0.astype(jnp.float32)[:, None]

    def fold(x):
        s = jnp.sum(x, axis=1)
        return s[:, :chans] + s[:, chans:]

    def spread(x):
        return jnp.concatenate([x, x], axis=1)[:, None, :]

    mean0 = fold(pre0 * mask0) / count0
    centred = (pre0 - spread(mean0)) * mask0
    var0 = fold(centred * centred) / count0
    inv_std = spread(lax.rsqrt(var0 + 1e-05))
    normed = centred * inv_std
    gain2 = jnp.concatenate([norm_gain, norm_gain])
    bias2 = jnp.concatenate([norm_bias, norm_bias])
    lifted = normed * gain2 + bias2
    act0 = (jax.nn.gelu(lifted, approximate=False) * mask0).astype(jnp.bfloat16)
    taps = jnp.concatenate([act0[:, :frames1], act0[:, 1 : frames1 + 1, :chans]], axis=2)
    kernel = w_second.reshape(taps_second * chans, chans)
    pre1 = jnp.einsum("rui,io->ruo", taps, kernel, preferred_element_type=jnp.float32)
    valid1 = (valid0 - taps_second) // 2 + 1
    mask1 = (jnp.arange(frames1, dtype=jnp.int32)[None, :] < valid1[:, None]).astype(jnp.float32)[
        :, :, None
    ]
    features = (jax.nn.gelu(pre1, approximate=False) * mask1).astype(jnp.bfloat16)
    grad1 = (cot.astype(jnp.float32) * gelu_slope(pre1) * mask1).astype(jnp.bfloat16)
    members = lax.axis_size("dev")
    width = chans // members
    grad_kernel = jnp.einsum("ruo,rui->oi", grad1, taps, preferred_element_type=jnp.float32)
    grad_kernel = grad_kernel.reshape(members, 2, width // 2, -1).transpose(1, 0, 2, 3)
    back = jnp.einsum("ruo,io->rui", grad1, kernel, preferred_element_type=jnp.float32)
    dact0 = jnp.pad(back[:, :, : 2 * chans], ((0, 0), (0, pairs - frames1), (0, 0))) + jnp.pad(
        back[:, :, 2 * chans :], ((0, 0), (1, pairs - frames1 - 1), (0, chans))
    )
    dlift = dact0 * gelu_slope(lifted) * mask0
    gain_terms = jnp.sum(dlift * normed, axis=(0, 1))
    bias_terms = jnp.sum(dlift, axis=(0, 1))
    grad_gain = gain_terms[:chans] + gain_terms[chans:]
    grad_bias = bias_terms[:chans] + bias_terms[chans:]
    dnorm = dlift * gain2
    first_mean = spread(fold(dnorm) / count0)
    second_mean = spread(fold(dnorm * normed) / count0)
    dpre0 = inv_std * (dnorm - first_mean - normed * second_mean) * mask0
    high = dpre0.astype(jnp.bfloat16)
    low = (dpre0 - high.astype(jnp.float32)).astype(jnp.bfloat16)
    grad_pair = jnp.einsum(
        "ruj,rum->jm", high, patches, preferred_element_type=jnp.float32
    ) + jnp.einsum("ruj,rum->jm", low, patches, preferred_element_type=jnp.float32)
    grad_filter = grad_pair[:chans, :ker_first] + grad_pair[chans:, stride_first:]
    small = jnp.concatenate([grad_filter, grad_gain[:, None], grad_bias[:, None]], axis=1)
    small = small.reshape(members, 2, width // 2, small.shape[1]).transpose(1, 0, 2, 3)
    grads = (grad_kernel, small)
    return (features, grads)


def shards(wave, lengths, order, w_first, norm_gain, norm_bias, w_second, cot):
    members = lax.axis_size("dev")
    member = lax.axis_index("dev")
    rows = wave.shape[0]
    share = rows // members
    own_order = lax.dynamic_index_in_dim(order, member, 0, keepdims=False)
    dealt = own_order.reshape(share, members).T.reshape(rows)
    outgoing = jnp.take(wave, dealt, axis=0)
    arrived = lax.all_to_all(outgoing, "dev", split_axis=0, concat_axis=0, tiled=True)
    picks = lax.dynamic_index_in_dim(
        order.reshape(members, share, members), member, 2, keepdims=False
    )
    slots = jnp.arange(rows, dtype=jnp.int32)
    hits = picks[:, :, None] == slots[None, None, :]
    lens = jnp.sum(
        jnp.where(hits, lengths.reshape(members, 1, rows), 0), axis=2, dtype=jnp.int32
    ).reshape(rows)
    features, (grad_kernel, small) = local_pass(
        arrived, lens, w_first, norm_gain, norm_bias, w_second, cot
    )
    taps_second = w_second.shape[0]
    in_chans = w_second.shape[1]
    ker_first = w_first.shape[0]
    members = lax.axis_size("dev")
    groups = lax.axis_size("grp")
    core = lax.rem(lax.axis_index("grp"), 2)
    pairs = [(g, g ^ 1) for g in range(groups)]

    def pair_sum(halves):
        keep = lax.dynamic_index_in_dim(halves, core, 0, keepdims=False)
        give = lax.dynamic_index_in_dim(halves, 1 - core, 0, keepdims=False)
        return keep + lax.ppermute(give, "grp", pairs)

    mine_kernel = pair_sum(grad_kernel).astype(jnp.bfloat16)
    mine_small = pair_sum(small)
    pieces_kernel, pieces_small = exchange(
        [mine_kernel, mine_small], members, "dev", 1, False, 0
    )
    part = jnp.concatenate(
        [jnp.sum(pieces_kernel.astype(jnp.float32), axis=0), jnp.sum(pieces_small, axis=0)],
        axis=1,
    )
    chans = w_second.shape[2]
    width = chans // members
    span = part.shape[1]
    rows_y = groups // 2
    gathered = reduce_gather(part.reshape(rows_y, (width // 2) // rows_y, span), 1)
    gathered = gathered.reshape(rows_y, 2, (width // 2) // rows_y, span)
    owned = gathered.transpose(1, 0, 2, 3).reshape(width, span)
    grad_second = (
        owned[:, : taps_second * in_chans].reshape(width, taps_second, in_chans).transpose(1, 2, 0)
    )
    grad_first = owned[:, taps_second * in_chans : taps_second * in_chans + ker_first].T
    grad_gain = owned[:, taps_second * in_chans + ker_first]
    grad_bias = owned[:, taps_second * in_chans + ker_first + 1]
    return (features, grad_second, grad_first, grad_gain, grad_bias)


def solution(mesh):
    placed = (
        P(("grp", "dev"), None),
        P("grp"),
        P("grp", None),
        P(),
        P(),
        P(),
        P(),
        P(("grp", "dev"), None, None),
    )
    return jax.shard_map(
        shards,
        mesh=mesh,
        in_specs=placed,
        out_specs=(
            P(("grp", "dev"), None, None),
            P(None, None, "dev"),
            P(None, "dev"),
            P("dev"),
            P("dev"),
        ),
        check_vma=False,
    )
```

```python
import functools

import jax
import jax.numpy as jnp
from jax import lax
from jax.experimental import pallas as pl
from jax.experimental.pallas import tpu as pltpu
from jax.sharding import PartitionSpec as P

MESH = pl.DeviceIdType.MESH


def exchange_kernel(members, axis, stride, gather, count, *refs):
    srcs = refs[:count]
    dsts = refs[count : 2 * count]
    send_sems, recv_sems, local_sems = refs[2 * count :]
    if axis == "grp":
        coord = lax.axis_index("grp")
        me = coord // stride
        offset = lax.rem(coord, stride)
        other = lax.axis_index("dev")
    else:
        me = lax.axis_index("dev")
        other = lax.axis_index("grp")

    def where(peer):
        return (peer * stride + offset, other) if axis == "grp" else (other, peer)

    def source(a, peer):
        return srcs[a].at[0] if gather else srcs[a].at[peer]

    def remote(a, step, peer, src_peer, slot):
        return pltpu.make_async_remote_copy(
            src_ref=source(a, src_peer),
            dst_ref=dsts[a].at[slot],
            send_sem=send_sems.at[a, step],
            recv_sem=recv_sems.at[a, step],
            device_id=where(peer),
            device_id_type=MESH,
        )

    barrier = pltpu.get_barrier_semaphore()

    def greet(step, carry):
        peer = lax.rem(me + step, members)
        pl.semaphore_signal(barrier, inc=1, device_id=where(peer), device_id_type=MESH)
        return carry

    lax.fori_loop(1, members, greet, 0)
    pl.semaphore_wait(barrier, members - 1)
    locals_ = [
        pltpu.make_async_copy(source(a, me), dsts[a].at[me], local_sems.at[a]) for a in range(count)
    ]
    for local in locals_:
        local.start()

    def send(step, carry):
        peer = lax.rem(me + step, members)
        for a in range(count):
            remote(a, step, peer, peer, me).start()
        return carry

    lax.fori_loop(1, members, send, 0)

    def finish(step, carry):
        peer = lax.rem(me + step, members)
        sender = lax.rem(me + members - step, members)
        for a in range(count):
            remote(a, step, peer, peer, me).wait_send()
            remote(a, step, sender, me, sender).wait_recv()
        return carry

    lax.fori_loop(1, members, finish, 0)
    for local in locals_:
        local.wait()


def exchange(blocks, members, axis, stride, gather, ident):
    count = len(blocks)
    shapes = [jax.ShapeDtypeStruct((members,) + b.shape[1:], b.dtype) for b in blocks]
    return pl.pallas_call(
        functools.partial(exchange_kernel, members, axis, stride, gather, count),
        out_shape=shapes,
        in_specs=[pl.BlockSpec(memory_space=pl.ANY)] * count,
        out_specs=[pl.BlockSpec(memory_space=pl.ANY)] * count,
        scratch_shapes=[
            pltpu.SemaphoreType.DMA((count, members)),
            pltpu.SemaphoreType.DMA((count, members)),
            pltpu.SemaphoreType.DMA((count,)),
        ],
        compiler_params=pltpu.CompilerParams(collective_id=ident, has_side_effects=True),
    )(*blocks)


def reduce_gather_kernel(rows_y, src_ref, out_ref, stage, total, sends, recvs, shares, gets, local_sems):
    coord = lax.axis_index("grp")
    other = lax.axis_index("dev")
    groups = 2 * rows_y
    me = coord // 2
    core = lax.rem(coord, 2)
    barrier = pltpu.get_barrier_semaphore()

    def greet(step, carry):
        peer = lax.rem(coord + step, groups)
        pl.semaphore_signal(barrier, inc=1, device_id=(peer, other), device_id_type=MESH)
        return carry

    lax.fori_loop(1, groups, greet, 0)
    pl.semaphore_wait(barrier, groups - 1)
    own = pltpu.make_async_copy(src_ref.at[me], stage.at[me], local_sems.at[0])
    own.start()

    def scatter(step, peer, src_peer, slot):
        return pltpu.make_async_remote_copy(
            src_ref=src_ref.at[src_peer],
            dst_ref=stage.at[slot],
            send_sem=sends.at[step],
            recv_sem=recvs.at[step],
            device_id=(peer * 2 + core, other),
            device_id_type=MESH,
        )

    def send_part(step, carry):
        peer = lax.rem(me + step, rows_y)
        scatter(step, peer, peer, me).start()
        return carry

    lax.fori_loop(1, rows_y, send_part, 0)

    def finish_part(step, carry):
        peer = lax.rem(me + step, rows_y)
        sender = lax.rem(me + rows_y - step, rows_y)
        scatter(step, peer, peer, me).wait_send()
        scatter(step, sender, me, sender).wait_recv()
        return carry

    lax.fori_loop(1, rows_y, finish_part, 0)
    own.wait()
    total[...] = jnp.sum(stage[...], axis=0)
    mine = pltpu.make_async_copy(total, out_ref.at[coord], local_sems.at[1])
    mine.start()

    def spread(step, peer, slot):
        return pltpu.make_async_remote_copy(
            src_ref=total,
            dst_ref=out_ref.at[slot],
            send_sem=shares.at[step],
            recv_sem=gets.at[step],
            device_id=(peer, other),
            device_id_type=MESH,
        )

    def send_total(step, carry):
        spread(step, lax.rem(coord + step, groups), coord).start()
        return carry

    lax.fori_loop(1, groups, send_total, 0)

    def finish_total(step, carry):
        spread(step, lax.rem(coord + step, groups), coord).wait_send()
        sender = lax.rem(coord + groups - step, groups)
        spread(step, sender, sender).wait_recv()
        return carry

    lax.fori_loop(1, groups, finish_total, 0)
    mine.wait()


def reduce_gather(part, ident):
    rows_y, depth, span = part.shape
    groups = 2 * rows_y
    return pl.pallas_call(
        functools.partial(reduce_gather_kernel, rows_y),
        out_shape=jax.ShapeDtypeStruct((groups, depth, span), part.dtype),
        in_specs=[pl.BlockSpec(memory_space=pl.ANY)],
        out_specs=pl.BlockSpec(memory_space=pl.ANY),
        scratch_shapes=[
            pltpu.VMEM((rows_y, depth, span), part.dtype),
            pltpu.VMEM((depth, span), part.dtype),
            pltpu.SemaphoreType.DMA((rows_y,)),
            pltpu.SemaphoreType.DMA((rows_y,)),
            pltpu.SemaphoreType.DMA((groups,)),
            pltpu.SemaphoreType.DMA((groups,)),
            pltpu.SemaphoreType.DMA((2,)),
        ],
        compiler_params=pltpu.CompilerParams(collective_id=ident, has_side_effects=True),
    )(part)


def gelu_slope(value):
    return (
        0.5 * (1.0 + lax.erf(value * 0.7071067811865476))
        + value * jnp.exp(-0.5 * value * value) * 0.3989422804014327
    )


def slope_from(value, cdf):
    return cdf + value * jnp.exp(-0.5 * value * value) * 0.3989422804014327


def local_pass(wave, lens, w_first, norm_gain, norm_bias, w_second, cot):
    rows, samp = wave.shape
    ker_first = w_first.shape[0]
    stride_first = ker_first // 2
    chans = w_first.shape[1]
    taps_second = w_second.shape[0]
    frames0 = (samp - ker_first) // stride_first + 1
    frames1 = (frames0 - taps_second) // 2 + 1
    pairs = (frames0 + 1) // 2
    hop = 2 * stride_first
    reach = hop + stride_first
    padded = jnp.pad(wave, ((0, 0), (0, hop * (pairs + 1) - samp)))
    blocks = padded.reshape(rows, pairs + 1, hop)
    patches = jnp.concatenate([blocks[:, :-1], blocks[:, 1:, :stride_first]], axis=2)
    zeros_w = jnp.zeros((stride_first, chans), w_first.dtype)
    w_pair = jnp.concatenate(
        [
            jnp.concatenate([w_first, zeros_w], axis=0),
            jnp.concatenate([zeros_w, w_first], axis=0),
        ],
        axis=1,
    )
    pre0 = jnp.einsum("rum,mc->ruc", patches, w_pair, preferred_element_type=jnp.float32)
    valid0 = (lens - ker_first) // stride_first + 1
    frame = (
        2 * jnp.arange(pairs, dtype=jnp.int32)[:, None]
        + (jnp.arange(2 * chans, dtype=jnp.int32) // chans)[None, :]
    )
    mask0 = (frame[None] < valid0[:, None, None]).astype(jnp.float32)
    count0 = valid0.astype(jnp.float32)[:, None]

    def fold(x):
        s = jnp.sum(x, axis=1)
        return s[:, :chans] + s[:, chans:]

    def spread(x):
        return jnp.concatenate([x, x], axis=1)[:, None, :]

    mean0 = fold(pre0 * mask0) / count0
    centred = (pre0 - spread(mean0)) * mask0
    var0 = fold(centred * centred) / count0
    inv_std = spread(lax.rsqrt(var0 + 1e-05))
    normed = centred * inv_std
    gain2 = jnp.concatenate([norm_gain, norm_gain])
    bias2 = jnp.concatenate([norm_bias, norm_bias])
    lifted = normed * gain2 + bias2
    cdf0 = 0.5 * (1.0 + lax.erf(lifted * 0.7071067811865476))
    act0 = (lifted * cdf0 * mask0).astype(jnp.bfloat16)
    taps = jnp.concatenate([act0[:, :frames1], act0[:, 1 : frames1 + 1, :chans]], axis=2)
    kernel = w_second.reshape(taps_second * chans, chans)
    pre1 = jnp.einsum("rui,io->ruo", taps, kernel, preferred_element_type=jnp.float32)
    valid1 = (valid0 - taps_second) // 2 + 1
    mask1 = (jnp.arange(frames1, dtype=jnp.int32)[None, :] < valid1[:, None]).astype(jnp.float32)[
        :, :, None
    ]
    cdf1 = 0.5 * (1.0 + lax.erf(pre1 * 0.7071067811865476))
    features = (pre1 * cdf1 * mask1).astype(jnp.bfloat16)
    grad1 = (cot.astype(jnp.float32) * slope_from(pre1, cdf1) * mask1).astype(jnp.bfloat16)
    members = lax.axis_size("dev")
    width = chans // members
    grad_kernel = jnp.einsum("ruo,rui->oi", grad1, taps, preferred_element_type=jnp.float32)
    grad_kernel = grad_kernel.reshape(members, 2, width // 2, -1).transpose(1, 0, 2, 3)
    back = jnp.einsum("ruo,io->rui", grad1, kernel, preferred_element_type=jnp.float32)
    dact0 = jnp.pad(back[:, :, : 2 * chans], ((0, 0), (0, pairs - frames1), (0, 0))) + jnp.pad(
        back[:, :, 2 * chans :], ((0, 0), (1, pairs - frames1 - 1), (0, chans))
    )
    dlift = dact0 * slope_from(lifted, cdf0) * mask0
    gain_terms = jnp.sum(dlift * normed, axis=(0, 1))
    bias_terms = jnp.sum(dlift, axis=(0, 1))
    grad_gain = gain_terms[:chans] + gain_terms[chans:]
    grad_bias = bias_terms[:chans] + bias_terms[chans:]
    dnorm = dlift * gain2
    first_mean = spread(fold(dnorm) / count0)
    second_mean = spread(fold(dnorm * normed) / count0)
    dpre0 = inv_std * (dnorm - first_mean - normed * second_mean) * mask0
    high = dpre0.astype(jnp.bfloat16)
    low = (dpre0 - high.astype(jnp.float32)).astype(jnp.bfloat16)
    grad_pair = jnp.einsum(
        "ruj,rum->jm", high, patches, preferred_element_type=jnp.float32
    ) + jnp.einsum("ruj,rum->jm", low, patches, preferred_element_type=jnp.float32)
    grad_filter = grad_pair[:chans, :ker_first] + grad_pair[chans:, stride_first:]
    small = jnp.concatenate([grad_filter, grad_gain[:, None], grad_bias[:, None]], axis=1)
    small = small.reshape(members, 2, width // 2, small.shape[1]).transpose(1, 0, 2, 3)
    grads = (grad_kernel, small)
    return (features, grads)


def shards(wave, lengths, order, w_first, norm_gain, norm_bias, w_second, cot):
    members = lax.axis_size("dev")
    member = lax.axis_index("dev")
    rows = wave.shape[0]
    share = rows // members
    own_order = lax.dynamic_index_in_dim(order, member, 0, keepdims=False)
    dealt = own_order.reshape(share, members).T.reshape(rows)
    outgoing = jnp.take(wave, dealt, axis=0)
    (arrived,) = exchange([outgoing.reshape(members, share, -1)], members, "dev", 1, False, 3)
    arrived = arrived.reshape(rows, -1)
    picks = lax.dynamic_index_in_dim(
        order.reshape(members, share, members), member, 2, keepdims=False
    )
    slots = jnp.arange(rows, dtype=jnp.int32)
    hits = picks[:, :, None] == slots[None, None, :]
    lens = jnp.sum(
        jnp.where(hits, lengths.reshape(members, 1, rows), 0), axis=2, dtype=jnp.int32
    ).reshape(rows)
    features, (grad_kernel, small) = local_pass(
        arrived, lens, w_first, norm_gain, norm_bias, w_second, cot
    )
    taps_second = w_second.shape[0]
    in_chans = w_second.shape[1]
    ker_first = w_first.shape[0]
    members = lax.axis_size("dev")
    groups = lax.axis_size("grp")
    core = lax.rem(lax.axis_index("grp"), 2)
    pairs = [(g, g ^ 1) for g in range(groups)]

    def pair_sum(halves):
        keep = lax.dynamic_index_in_dim(halves, core, 0, keepdims=False)
        give = lax.dynamic_index_in_dim(halves, 1 - core, 0, keepdims=False)
        return keep + lax.ppermute(give, "grp", pairs)

    mine_kernel = pair_sum(grad_kernel).astype(jnp.bfloat16)
    mine_small = pair_sum(small)
    pieces_kernel, pieces_small = exchange(
        [mine_kernel, mine_small], members, "dev", 1, False, 0
    )
    part = jnp.concatenate(
        [jnp.sum(pieces_kernel.astype(jnp.float32), axis=0), jnp.sum(pieces_small, axis=0)],
        axis=1,
    )
    chans = w_second.shape[2]
    width = chans // members
    span = part.shape[1]
    rows_y = groups // 2
    gathered = reduce_gather(part.reshape(rows_y, (width // 2) // rows_y, span), 1)
    gathered = gathered.reshape(rows_y, 2, (width // 2) // rows_y, span)
    owned = gathered.transpose(1, 0, 2, 3).reshape(width, span)
    grad_second = (
        owned[:, : taps_second * in_chans].reshape(width, taps_second, in_chans).transpose(1, 2, 0)
    )
    grad_first = owned[:, taps_second * in_chans : taps_second * in_chans + ker_first].T
    grad_gain = owned[:, taps_second * in_chans + ker_first]
    grad_bias = owned[:, taps_second * in_chans + ker_first + 1]
    return (features, grad_second, grad_first, grad_gain, grad_bias)


def solution(mesh):
    placed = (
        P(("grp", "dev"), None),
        P("grp"),
        P("grp", None),
        P(),
        P(),
        P(),
        P(),
        P(("grp", "dev"), None, None),
    )
    return jax.shard_map(
        shards,
        mesh=mesh,
        in_specs=placed,
        out_specs=(
            P(("grp", "dev"), None, None),
            P(None, None, "dev"),
            P(None, "dev"),
            P("dev"),
            P("dev"),
        ),
        check_vma=False,
    )
```

```python
import functools

import jax
import jax.numpy as jnp
from jax import lax
from jax.experimental import pallas as pl
from jax.experimental.pallas import tpu as pltpu
from jax.sharding import PartitionSpec as P

MESH = pl.DeviceIdType.MESH


def exchange_kernel(members, axis, stride, gather, count, *refs):
    srcs = refs[:count]
    dsts = refs[count : 2 * count]
    send_sems, recv_sems, local_sems = refs[2 * count :]
    if axis == "grp":
        coord = lax.axis_index("grp")
        me = coord // stride
        offset = lax.rem(coord, stride)
        other = lax.axis_index("dev")
    else:
        me = lax.axis_index("dev")
        other = lax.axis_index("grp")

    def where(peer):
        return (peer * stride + offset, other) if axis == "grp" else (other, peer)

    def source(a, peer):
        return srcs[a].at[0] if gather else srcs[a].at[peer]

    def remote(a, step, peer, src_peer, slot):
        return pltpu.make_async_remote_copy(
            src_ref=source(a, src_peer),
            dst_ref=dsts[a].at[slot],
            send_sem=send_sems.at[a, step],
            recv_sem=recv_sems.at[a, step],
            device_id=where(peer),
            device_id_type=MESH,
        )

    barrier = pltpu.get_barrier_semaphore()

    def greet(step, carry):
        peer = lax.rem(me + step, members)
        pl.semaphore_signal(barrier, inc=1, device_id=where(peer), device_id_type=MESH)
        return carry

    lax.fori_loop(1, members, greet, 0)
    pl.semaphore_wait(barrier, members - 1)
    locals_ = [
        pltpu.make_async_copy(source(a, me), dsts[a].at[me], local_sems.at[a]) for a in range(count)
    ]
    for local in locals_:
        local.start()

    def send(step, carry):
        peer = lax.rem(me + step, members)
        for a in range(count):
            remote(a, step, peer, peer, me).start()
        return carry

    lax.fori_loop(1, members, send, 0)

    def finish(step, carry):
        peer = lax.rem(me + step, members)
        sender = lax.rem(me + members - step, members)
        for a in range(count):
            remote(a, step, peer, peer, me).wait_send()
            remote(a, step, sender, me, sender).wait_recv()
        return carry

    lax.fori_loop(1, members, finish, 0)
    for local in locals_:
        local.wait()


def exchange(blocks, members, axis, stride, gather, ident):
    count = len(blocks)
    shapes = [jax.ShapeDtypeStruct((members,) + b.shape[1:], b.dtype) for b in blocks]
    return pl.pallas_call(
        functools.partial(exchange_kernel, members, axis, stride, gather, count),
        out_shape=shapes,
        in_specs=[pl.BlockSpec(memory_space=pl.ANY)] * count,
        out_specs=[pl.BlockSpec(memory_space=pl.ANY)] * count,
        scratch_shapes=[
            pltpu.SemaphoreType.DMA((count, members)),
            pltpu.SemaphoreType.DMA((count, members)),
            pltpu.SemaphoreType.DMA((count,)),
        ],
        compiler_params=pltpu.CompilerParams(collective_id=ident, has_side_effects=True),
    )(*blocks)


def reduce_gather_kernel(rows_y, src_ref, out_ref, stage, total, sends, recvs, shares, gets, local_sems):
    coord = lax.axis_index("grp")
    other = lax.axis_index("dev")
    groups = 2 * rows_y
    me = coord // 2
    core = lax.rem(coord, 2)
    barrier = pltpu.get_barrier_semaphore()

    def greet(step, carry):
        peer = lax.rem(coord + step, groups)
        pl.semaphore_signal(barrier, inc=1, device_id=(peer, other), device_id_type=MESH)
        return carry

    lax.fori_loop(1, groups, greet, 0)
    pl.semaphore_wait(barrier, groups - 1)
    own = pltpu.make_async_copy(src_ref.at[me], stage.at[me], local_sems.at[0])
    own.start()

    def scatter(step, peer, src_peer, slot):
        return pltpu.make_async_remote_copy(
            src_ref=src_ref.at[src_peer],
            dst_ref=stage.at[slot],
            send_sem=sends.at[step],
            recv_sem=recvs.at[step],
            device_id=(peer * 2 + core, other),
            device_id_type=MESH,
        )

    def send_part(step, carry):
        peer = lax.rem(me + step, rows_y)
        scatter(step, peer, peer, me).start()
        return carry

    lax.fori_loop(1, rows_y, send_part, 0)

    def finish_part(step, carry):
        peer = lax.rem(me + step, rows_y)
        sender = lax.rem(me + rows_y - step, rows_y)
        scatter(step, peer, peer, me).wait_send()
        scatter(step, sender, me, sender).wait_recv()
        return carry

    lax.fori_loop(1, rows_y, finish_part, 0)
    own.wait()
    total[...] = jnp.sum(stage[...], axis=0)
    mine = pltpu.make_async_copy(total, out_ref.at[coord], local_sems.at[1])
    mine.start()

    def spread(step, peer, slot):
        return pltpu.make_async_remote_copy(
            src_ref=total,
            dst_ref=out_ref.at[slot],
            send_sem=shares.at[step],
            recv_sem=gets.at[step],
            device_id=(peer, other),
            device_id_type=MESH,
        )

    def send_total(step, carry):
        spread(step, lax.rem(coord + step, groups), coord).start()
        return carry

    lax.fori_loop(1, groups, send_total, 0)

    def finish_total(step, carry):
        spread(step, lax.rem(coord + step, groups), coord).wait_send()
        sender = lax.rem(coord + groups - step, groups)
        spread(step, sender, sender).wait_recv()
        return carry

    lax.fori_loop(1, groups, finish_total, 0)
    mine.wait()


def reduce_gather(part, ident):
    rows_y, depth, span = part.shape
    groups = 2 * rows_y
    return pl.pallas_call(
        functools.partial(reduce_gather_kernel, rows_y),
        out_shape=jax.ShapeDtypeStruct((groups, depth, span), part.dtype),
        in_specs=[pl.BlockSpec(memory_space=pl.ANY)],
        out_specs=pl.BlockSpec(memory_space=pl.ANY),
        scratch_shapes=[
            pltpu.VMEM((rows_y, depth, span), part.dtype),
            pltpu.VMEM((depth, span), part.dtype),
            pltpu.SemaphoreType.DMA((rows_y,)),
            pltpu.SemaphoreType.DMA((rows_y,)),
            pltpu.SemaphoreType.DMA((groups,)),
            pltpu.SemaphoreType.DMA((groups,)),
            pltpu.SemaphoreType.DMA((2,)),
        ],
        compiler_params=pltpu.CompilerParams(collective_id=ident, has_side_effects=True),
    )(part)


def gelu_slope(value):
    return (
        0.5 * (1.0 + lax.erf(value * 0.7071067811865476))
        + value * jnp.exp(-0.5 * value * value) * 0.3989422804014327
    )


def slope_from(value, cdf):
    return cdf + value * jnp.exp(-0.5 * value * value) * 0.3989422804014327


def local_pass(wave, lens, w_first, norm_gain, norm_bias, w_second, cot):
    rows, samp = wave.shape
    ker_first = w_first.shape[0]
    stride_first = ker_first // 2
    chans = w_first.shape[1]
    taps_second = w_second.shape[0]
    frames0 = (samp - ker_first) // stride_first + 1
    frames1 = (frames0 - taps_second) // 2 + 1
    pairs = (frames0 + 1) // 2
    hop = 2 * stride_first
    reach = hop + stride_first
    padded = jnp.pad(wave, ((0, 0), (0, hop * (pairs + 1) - samp)))
    blocks = padded.reshape(rows, pairs + 1, hop)
    patches = jnp.concatenate([blocks[:, :-1], blocks[:, 1:, :stride_first]], axis=2)
    zeros_w = jnp.zeros((stride_first, chans), w_first.dtype)
    w_pair = jnp.concatenate(
        [
            jnp.concatenate([w_first, zeros_w], axis=0),
            jnp.concatenate([zeros_w, w_first], axis=0),
        ],
        axis=1,
    )
    pre0 = jnp.einsum("rum,mc->ruc", patches, w_pair, preferred_element_type=jnp.float32)
    valid0 = (lens - ker_first) // stride_first + 1
    frame = (
        2 * jnp.arange(pairs, dtype=jnp.int32)[:, None]
        + (jnp.arange(2 * chans, dtype=jnp.int32) // chans)[None, :]
    )
    mask0 = (frame[None] < valid0[:, None, None]).astype(jnp.float32)
    count0 = valid0.astype(jnp.float32)[:, None]

    def fold(x):
        s = jnp.sum(x, axis=1)
        return s[:, :chans] + s[:, chans:]

    def spread(x):
        return jnp.concatenate([x, x], axis=1)[:, None, :]

    mean0 = fold(pre0 * mask0) / count0
    centred = (pre0 - spread(mean0)) * mask0
    var0 = fold(centred * centred) / count0
    inv_std = spread(lax.rsqrt(var0 + 1e-05))
    normed = centred * inv_std
    gain2 = jnp.concatenate([norm_gain, norm_gain])
    bias2 = jnp.concatenate([norm_bias, norm_bias])
    lifted = normed * gain2 + bias2
    cdf0 = 0.5 * (1.0 + lax.erf(lifted * 0.7071067811865476))
    act0 = (lifted * cdf0 * mask0).astype(jnp.bfloat16)
    taps = jnp.concatenate([act0[:, :frames1], act0[:, 1 : frames1 + 1, :chans]], axis=2)
    kernel = w_second.reshape(taps_second * chans, chans)
    pre1 = jnp.einsum("rui,io->ruo", taps, kernel, preferred_element_type=jnp.float32)
    valid1 = (valid0 - taps_second) // 2 + 1
    mask1 = (jnp.arange(frames1, dtype=jnp.int32)[None, :] < valid1[:, None]).astype(jnp.float32)[
        :, :, None
    ]
    cdf1 = 0.5 * (1.0 + lax.erf(pre1 * 0.7071067811865476))
    features = (pre1 * cdf1 * mask1).astype(jnp.bfloat16)
    grad1 = (cot.astype(jnp.float32) * slope_from(pre1, cdf1) * mask1).astype(jnp.bfloat16)
    members = lax.axis_size("dev")
    width = chans // members
    grad_kernel = jnp.einsum("ruo,rui->oi", grad1, taps, preferred_element_type=jnp.float32)
    grad_kernel = grad_kernel.reshape(members, 2, width // 2, -1).transpose(1, 0, 2, 3)
    back = jnp.einsum("ruo,io->rui", grad1, kernel, preferred_element_type=jnp.float32)
    dact0 = jnp.pad(back[:, :, : 2 * chans], ((0, 0), (0, pairs - frames1), (0, 0))) + jnp.pad(
        back[:, :, 2 * chans :], ((0, 0), (1, pairs - frames1 - 1), (0, chans))
    )
    dlift = dact0 * slope_from(lifted, cdf0) * mask0
    gain_terms = jnp.sum(dlift * normed, axis=(0, 1))
    bias_terms = jnp.sum(dlift, axis=(0, 1))
    grad_gain = gain_terms[:chans] + gain_terms[chans:]
    grad_bias = bias_terms[:chans] + bias_terms[chans:]
    dnorm = dlift * gain2
    first_mean = spread(fold(dnorm) / count0)
    second_mean = spread(fold(dnorm * normed) / count0)
    dpre0 = inv_std * (dnorm - first_mean - normed * second_mean) * mask0
    high = dpre0.astype(jnp.bfloat16)
    low = (dpre0 - high.astype(jnp.float32)).astype(jnp.bfloat16)
    grad_pair = jnp.einsum(
        "rum,ruj->mj", patches, high, preferred_element_type=jnp.float32
    ) + jnp.einsum("rum,ruj->mj", patches, low, preferred_element_type=jnp.float32)
    grad_filter = (grad_pair[:ker_first, :chans] + grad_pair[stride_first:, chans:]).T
    small = jnp.concatenate([grad_filter, grad_gain[:, None], grad_bias[:, None]], axis=1)
    small = small.reshape(members, 2, width // 2, small.shape[1]).transpose(1, 0, 2, 3)
    grads = (grad_kernel, small)
    return (features, grads)


def shards(wave, lengths, order, w_first, norm_gain, norm_bias, w_second, cot):
    members = lax.axis_size("dev")
    member = lax.axis_index("dev")
    rows = wave.shape[0]
    share = rows // members
    own_order = lax.dynamic_index_in_dim(order, member, 0, keepdims=False)
    dealt = own_order.reshape(share, members).T.reshape(rows)
    outgoing = jnp.take(wave, dealt, axis=0)
    (arrived,) = exchange([outgoing.reshape(members, share, -1)], members, "dev", 1, False, 3)
    arrived = arrived.reshape(rows, -1)
    picks = lax.dynamic_index_in_dim(
        order.reshape(members, share, members), member, 2, keepdims=False
    )
    slots = jnp.arange(rows, dtype=jnp.int32)
    hits = picks[:, :, None] == slots[None, None, :]
    lens = jnp.sum(
        jnp.where(hits, lengths.reshape(members, 1, rows), 0), axis=2, dtype=jnp.int32
    ).reshape(rows)
    features, (grad_kernel, small) = local_pass(
        arrived, lens, w_first, norm_gain, norm_bias, w_second, cot
    )
    taps_second = w_second.shape[0]
    in_chans = w_second.shape[1]
    ker_first = w_first.shape[0]
    members = lax.axis_size("dev")
    groups = lax.axis_size("grp")
    core = lax.rem(lax.axis_index("grp"), 2)
    pairs = [(g, g ^ 1) for g in range(groups)]

    def pair_sum(halves):
        keep = lax.dynamic_index_in_dim(halves, core, 0, keepdims=False)
        give = lax.dynamic_index_in_dim(halves, 1 - core, 0, keepdims=False)
        return keep + lax.ppermute(give, "grp", pairs)

    mine_kernel = pair_sum(grad_kernel).astype(jnp.bfloat16)
    mine_small = pair_sum(small)
    pieces_kernel, pieces_small = exchange(
        [mine_kernel, mine_small], members, "dev", 1, False, 0
    )
    part = jnp.concatenate(
        [jnp.sum(pieces_kernel.astype(jnp.float32), axis=0), jnp.sum(pieces_small, axis=0)],
        axis=1,
    )
    chans = w_second.shape[2]
    width = chans // members
    span = part.shape[1]
    rows_y = groups // 2
    gathered = reduce_gather(part.reshape(rows_y, (width // 2) // rows_y, span), 1)
    gathered = gathered.reshape(rows_y, 2, (width // 2) // rows_y, span)
    owned = gathered.transpose(1, 0, 2, 3).reshape(width, span)
    grad_second = (
        owned[:, : taps_second * in_chans].reshape(width, taps_second, in_chans).transpose(1, 2, 0)
    )
    grad_first = owned[:, taps_second * in_chans : taps_second * in_chans + ker_first].T
    grad_gain = owned[:, taps_second * in_chans + ker_first]
    grad_bias = owned[:, taps_second * in_chans + ker_first + 1]
    return (features, grad_second, grad_first, grad_gain, grad_bias)


def solution(mesh):
    placed = (
        P(("grp", "dev"), None),
        P("grp"),
        P("grp", None),
        P(),
        P(),
        P(),
        P(),
        P(("grp", "dev"), None, None),
    )
    return jax.shard_map(
        shards,
        mesh=mesh,
        in_specs=placed,
        out_specs=(
            P(("grp", "dev"), None, None),
            P(None, None, "dev"),
            P(None, "dev"),
            P("dev"),
            P("dev"),
        ),
        check_vma=False,
    )
```

```python
import functools

import jax
import jax.numpy as jnp
from jax import lax
from jax.experimental import pallas as pl
from jax.experimental.pallas import tpu as pltpu
from jax.sharding import PartitionSpec as P

MESH = pl.DeviceIdType.MESH


def exchange_kernel(members, axis, stride, gather, count, *refs):
    srcs = refs[:count]
    dsts = refs[count : 2 * count]
    send_sems, recv_sems, local_sems = refs[2 * count :]
    if axis == "grp":
        coord = lax.axis_index("grp")
        me = coord // stride
        offset = lax.rem(coord, stride)
        other = lax.axis_index("dev")
    else:
        me = lax.axis_index("dev")
        other = lax.axis_index("grp")

    def where(peer):
        return (peer * stride + offset, other) if axis == "grp" else (other, peer)

    def source(a, peer):
        return srcs[a].at[0] if gather else srcs[a].at[peer]

    def remote(a, step, peer, src_peer, slot):
        return pltpu.make_async_remote_copy(
            src_ref=source(a, src_peer),
            dst_ref=dsts[a].at[slot],
            send_sem=send_sems.at[a, step],
            recv_sem=recv_sems.at[a, step],
            device_id=where(peer),
            device_id_type=MESH,
        )

    barrier = pltpu.get_barrier_semaphore()

    def greet(step, carry):
        peer = lax.rem(me + step, members)
        pl.semaphore_signal(barrier, inc=1, device_id=where(peer), device_id_type=MESH)
        return carry

    lax.fori_loop(1, members, greet, 0)
    pl.semaphore_wait(barrier, members - 1)
    locals_ = [
        pltpu.make_async_copy(source(a, me), dsts[a].at[me], local_sems.at[a]) for a in range(count)
    ]
    for local in locals_:
        local.start()

    def send(step, carry):
        peer = lax.rem(me + step, members)
        for a in range(count):
            remote(a, step, peer, peer, me).start()
        return carry

    lax.fori_loop(1, members, send, 0)

    def finish(step, carry):
        peer = lax.rem(me + step, members)
        sender = lax.rem(me + members - step, members)
        for a in range(count):
            remote(a, step, peer, peer, me).wait_send()
            remote(a, step, sender, me, sender).wait_recv()
        return carry

    lax.fori_loop(1, members, finish, 0)
    for local in locals_:
        local.wait()


def exchange(blocks, members, axis, stride, gather, ident):
    count = len(blocks)
    shapes = [jax.ShapeDtypeStruct((members,) + b.shape[1:], b.dtype) for b in blocks]
    return pl.pallas_call(
        functools.partial(exchange_kernel, members, axis, stride, gather, count),
        out_shape=shapes,
        in_specs=[pl.BlockSpec(memory_space=pl.ANY)] * count,
        out_specs=[pl.BlockSpec(memory_space=pl.ANY)] * count,
        scratch_shapes=[
            pltpu.SemaphoreType.DMA((count, members)),
            pltpu.SemaphoreType.DMA((count, members)),
            pltpu.SemaphoreType.DMA((count,)),
        ],
        compiler_params=pltpu.CompilerParams(collective_id=ident, has_side_effects=True),
    )(*blocks)


def reduce_gather_kernel(rows_y, src_ref, out_ref, stage, total, sends, recvs, shares, gets, local_sems):
    coord = lax.axis_index("grp")
    other = lax.axis_index("dev")
    groups = 2 * rows_y
    me = coord // 2
    core = lax.rem(coord, 2)
    barrier = pltpu.get_barrier_semaphore()

    def greet(step, carry):
        peer = lax.rem(coord + step, groups)
        pl.semaphore_signal(barrier, inc=1, device_id=(peer, other), device_id_type=MESH)
        return carry

    lax.fori_loop(1, groups, greet, 0)
    pl.semaphore_wait(barrier, groups - 1)
    own = pltpu.make_async_copy(src_ref.at[me], stage.at[me], local_sems.at[0])
    own.start()

    def scatter(step, peer, src_peer, slot):
        return pltpu.make_async_remote_copy(
            src_ref=src_ref.at[src_peer],
            dst_ref=stage.at[slot],
            send_sem=sends.at[step],
            recv_sem=recvs.at[step],
            device_id=(peer * 2 + core, other),
            device_id_type=MESH,
        )

    def send_part(step, carry):
        peer = lax.rem(me + step, rows_y)
        scatter(step, peer, peer, me).start()
        return carry

    lax.fori_loop(1, rows_y, send_part, 0)

    def finish_part(step, carry):
        peer = lax.rem(me + step, rows_y)
        sender = lax.rem(me + rows_y - step, rows_y)
        scatter(step, peer, peer, me).wait_send()
        scatter(step, sender, me, sender).wait_recv()
        return carry

    lax.fori_loop(1, rows_y, finish_part, 0)
    own.wait()
    total[...] = jnp.sum(stage[...], axis=0)
    mine = pltpu.make_async_copy(total, out_ref.at[coord], local_sems.at[1])
    mine.start()

    def spread(step, peer, slot):
        return pltpu.make_async_remote_copy(
            src_ref=total,
            dst_ref=out_ref.at[slot],
            send_sem=shares.at[step],
            recv_sem=gets.at[step],
            device_id=(peer, other),
            device_id_type=MESH,
        )

    def send_total(step, carry):
        spread(step, lax.rem(coord + step, groups), coord).start()
        return carry

    lax.fori_loop(1, groups, send_total, 0)

    def finish_total(step, carry):
        spread(step, lax.rem(coord + step, groups), coord).wait_send()
        sender = lax.rem(coord + groups - step, groups)
        spread(step, sender, sender).wait_recv()
        return carry

    lax.fori_loop(1, groups, finish_total, 0)
    mine.wait()


def reduce_gather(part, ident):
    rows_y, depth, span = part.shape
    groups = 2 * rows_y
    return pl.pallas_call(
        functools.partial(reduce_gather_kernel, rows_y),
        out_shape=jax.ShapeDtypeStruct((groups, depth, span), part.dtype),
        in_specs=[pl.BlockSpec(memory_space=pl.ANY)],
        out_specs=pl.BlockSpec(memory_space=pl.ANY),
        scratch_shapes=[
            pltpu.VMEM((rows_y, depth, span), part.dtype),
            pltpu.VMEM((depth, span), part.dtype),
            pltpu.SemaphoreType.DMA((rows_y,)),
            pltpu.SemaphoreType.DMA((rows_y,)),
            pltpu.SemaphoreType.DMA((groups,)),
            pltpu.SemaphoreType.DMA((groups,)),
            pltpu.SemaphoreType.DMA((2,)),
        ],
        compiler_params=pltpu.CompilerParams(collective_id=ident, has_side_effects=True),
    )(part)


def gelu_slope(value):
    return (
        0.5 * (1.0 + lax.erf(value * 0.7071067811865476))
        + value * jnp.exp(-0.5 * value * value) * 0.3989422804014327
    )


def slope_from(value, cdf):
    return cdf + value * jnp.exp(-0.5 * value * value) * 0.3989422804014327


def local_pass(wave, lens, w_first, norm_gain, norm_bias, w_second, cot):
    rows, samp = wave.shape
    ker_first = w_first.shape[0]
    stride_first = ker_first // 2
    chans = w_first.shape[1]
    taps_second = w_second.shape[0]
    frames0 = (samp - ker_first) // stride_first + 1
    frames1 = (frames0 - taps_second) // 2 + 1
    pairs = (frames0 + 1) // 2
    hop = 2 * stride_first
    reach = hop + stride_first
    padded = jnp.pad(wave, ((0, 0), (0, hop * (pairs + 1) - samp)))
    blocks = padded.reshape(rows, pairs + 1, hop)
    patches = jnp.concatenate([blocks[:, :-1], blocks[:, 1:, :stride_first]], axis=2)
    zeros_w = jnp.zeros((stride_first, chans), w_first.dtype)
    w_pair = jnp.concatenate(
        [
            jnp.concatenate([w_first, zeros_w], axis=0),
            jnp.concatenate([zeros_w, w_first], axis=0),
        ],
        axis=1,
    )
    pre0 = jnp.einsum("rum,mc->ruc", patches, w_pair, preferred_element_type=jnp.float32)
    valid0 = (lens - ker_first) // stride_first + 1
    frame = (
        2 * jnp.arange(pairs, dtype=jnp.int32)[:, None]
        + (jnp.arange(2 * chans, dtype=jnp.int32) // chans)[None, :]
    )
    mask0 = (frame[None] < valid0[:, None, None]).astype(jnp.float32)
    count0 = valid0.astype(jnp.float32)[:, None]

    def fold(x):
        s = jnp.sum(x, axis=1)
        return s[:, :chans] + s[:, chans:]

    def spread(x):
        return jnp.concatenate([x, x], axis=1)[:, None, :]

    mean0 = fold(pre0 * mask0) / count0
    centred = (pre0 - spread(mean0)) * mask0
    var0 = fold(centred * centred) / count0
    inv_std = spread(lax.rsqrt(var0 + 1e-05))
    normed = centred * inv_std
    gain2 = jnp.concatenate([norm_gain, norm_gain])
    bias2 = jnp.concatenate([norm_bias, norm_bias])
    lifted = normed * gain2 + bias2
    cdf0 = 0.5 * (1.0 + lax.erf(lifted * 0.7071067811865476))
    act0 = (lifted * cdf0 * mask0).astype(jnp.bfloat16)
    taps = jnp.concatenate([act0[:, :frames1], act0[:, 1 : frames1 + 1, :chans]], axis=2)
    kernel = w_second.reshape(taps_second * chans, chans)
    pre1 = jnp.einsum("rui,io->ruo", taps, kernel, preferred_element_type=jnp.float32)
    valid1 = (valid0 - taps_second) // 2 + 1
    mask1 = (jnp.arange(frames1, dtype=jnp.int32)[None, :] < valid1[:, None]).astype(jnp.float32)[
        :, :, None
    ]
    cdf1 = 0.5 * (1.0 + lax.erf(pre1 * 0.7071067811865476))
    features = (pre1 * cdf1 * mask1).astype(jnp.bfloat16)
    grad1 = (cot.astype(jnp.float32) * slope_from(pre1, cdf1) * mask1).astype(jnp.bfloat16)
    members = lax.axis_size("dev")
    width = chans // members
    grad_kernel = jnp.einsum("ruo,rui->oi", grad1, taps, preferred_element_type=jnp.float32)
    grad_kernel = grad_kernel.reshape(members, 2, width // 2, -1).transpose(1, 0, 2, 3)
    back = jnp.einsum("ruo,io->rui", grad1, kernel, preferred_element_type=jnp.float32)
    dact0 = jnp.pad(back[:, :, : 2 * chans], ((0, 0), (0, pairs - frames1), (0, 0))) + jnp.pad(
        back[:, :, 2 * chans :], ((0, 0), (1, pairs - frames1 - 1), (0, chans))
    )
    dlift = dact0 * slope_from(lifted, cdf0) * mask0
    gain_terms = jnp.sum(dlift * normed, axis=(0, 1))
    bias_terms = jnp.sum(dlift, axis=(0, 1))
    grad_gain = gain_terms[:chans] + gain_terms[chans:]
    grad_bias = bias_terms[:chans] + bias_terms[chans:]
    dnorm = dlift * gain2
    first_mean = spread(fold(dnorm) / count0)
    second_mean = spread(fold(dnorm * normed) / count0)
    dpre0 = inv_std * (dnorm - first_mean - normed * second_mean) * mask0
    high = dpre0.astype(jnp.bfloat16)
    low = (dpre0 - high.astype(jnp.float32)).astype(jnp.bfloat16)
    grad_pair = jnp.einsum(
        "ruj,rum->jm", high, patches, preferred_element_type=jnp.float32
    ) + jnp.einsum("ruj,rum->jm", low, patches, preferred_element_type=jnp.float32)
    grad_filter = grad_pair[:chans, :ker_first] + grad_pair[chans:, stride_first:]
    small = jnp.concatenate([grad_filter, grad_gain[:, None], grad_bias[:, None]], axis=1)
    small = small.reshape(members, 2, width // 2, small.shape[1]).transpose(1, 0, 2, 3)
    grads = (grad_kernel, small)
    return (features, grads)


def shards(wave, lengths, order, w_first, norm_gain, norm_bias, w_second, cot):
    members = lax.axis_size("dev")
    member = lax.axis_index("dev")
    rows = wave.shape[0]
    share = rows // members
    own_order = lax.dynamic_index_in_dim(order, member, 0, keepdims=False)
    dealt = own_order.reshape(share, members).T.reshape(rows)
    outgoing = jnp.take(wave, dealt, axis=0)
    (arrived,) = exchange([outgoing.reshape(members, share, -1)], members, "dev", 1, False, 3)
    arrived = arrived.reshape(rows, -1)
    picks = lax.dynamic_index_in_dim(
        order.reshape(members, share, members), member, 2, keepdims=False
    )
    slots = jnp.arange(rows, dtype=jnp.int32)
    hits = picks[:, :, None] == slots[None, None, :]
    lens = jnp.sum(
        jnp.where(hits, lengths.reshape(members, 1, rows), 0), axis=2, dtype=jnp.int32
    ).reshape(rows)
    features, (grad_kernel, small) = local_pass(
        arrived, lens, w_first, norm_gain, norm_bias, w_second, cot
    )
    taps_second = w_second.shape[0]
    in_chans = w_second.shape[1]
    ker_first = w_first.shape[0]
    members = lax.axis_size("dev")
    groups = lax.axis_size("grp")
    core = lax.rem(lax.axis_index("grp"), 2)
    pairs = [(g, g ^ 1) for g in range(groups)]

    def pair_sum(halves):
        keep = lax.dynamic_index_in_dim(halves, core, 0, keepdims=False)
        give = lax.dynamic_index_in_dim(halves, 1 - core, 0, keepdims=False)
        return keep + lax.ppermute(give, "grp", pairs)

    mine_kernel = pair_sum(grad_kernel).astype(jnp.bfloat16)
    mine_small = pair_sum(small)
    small_high = mine_small.astype(jnp.bfloat16)
    small_low = (mine_small - small_high.astype(jnp.float32)).astype(jnp.bfloat16)
    (pieces,) = exchange(
        [jnp.concatenate([mine_kernel, small_high, small_low], axis=2)], members, "dev", 1, False, 0
    )
    sums = jnp.sum(pieces.astype(jnp.float32), axis=0)
    extra = small.shape[-1]
    lead = sums.shape[1] - 2 * extra
    part = jnp.concatenate(
        [sums[:, :lead], sums[:, lead : lead + extra] + sums[:, lead + extra :]], axis=1
    )
    chans = w_second.shape[2]
    width = chans // members
    span = part.shape[1]
    rows_y = groups // 2
    gathered = reduce_gather(part.reshape(rows_y, (width // 2) // rows_y, span), 1)
    gathered = gathered.reshape(rows_y, 2, (width // 2) // rows_y, span)
    owned = gathered.transpose(1, 0, 2, 3).reshape(width, span)
    grad_second = (
        owned[:, : taps_second * in_chans].reshape(width, taps_second, in_chans).transpose(1, 2, 0)
    )
    grad_first = owned[:, taps_second * in_chans : taps_second * in_chans + ker_first].T
    grad_gain = owned[:, taps_second * in_chans + ker_first]
    grad_bias = owned[:, taps_second * in_chans + ker_first + 1]
    return (features, grad_second, grad_first, grad_gain, grad_bias)


def solution(mesh):
    placed = (
        P(("grp", "dev"), None),
        P("grp"),
        P("grp", None),
        P(),
        P(),
        P(),
        P(),
        P(("grp", "dev"), None, None),
    )
    return jax.shard_map(
        shards,
        mesh=mesh,
        in_specs=placed,
        out_specs=(
            P(("grp", "dev"), None, None),
            P(None, None, "dev"),
            P(None, "dev"),
            P("dev"),
            P("dev"),
        ),
        check_vma=False,
    )
```

```python
import functools

import jax
import jax.numpy as jnp
from jax import lax
from jax.experimental import pallas as pl
from jax.experimental.pallas import tpu as pltpu
from jax.sharding import PartitionSpec as P

MESH = pl.DeviceIdType.MESH


def exchange_kernel(members, axis, stride, gather, count, *refs):
    srcs = refs[:count]
    dsts = refs[count : 2 * count]
    send_sems, recv_sems, local_sems = refs[2 * count :]
    if axis == "grp":
        coord = lax.axis_index("grp")
        me = coord // stride
        offset = lax.rem(coord, stride)
        other = lax.axis_index("dev")
    else:
        me = lax.axis_index("dev")
        other = lax.axis_index("grp")

    def where(peer):
        return (peer * stride + offset, other) if axis == "grp" else (other, peer)

    def source(a, peer):
        return srcs[a].at[0] if gather else srcs[a].at[peer]

    def remote(a, step, peer, src_peer, slot):
        return pltpu.make_async_remote_copy(
            src_ref=source(a, src_peer),
            dst_ref=dsts[a].at[slot],
            send_sem=send_sems.at[a, step],
            recv_sem=recv_sems.at[a, step],
            device_id=where(peer),
            device_id_type=MESH,
        )

    barrier = pltpu.get_barrier_semaphore()

    def greet(step, carry):
        peer = lax.rem(me + step, members)
        pl.semaphore_signal(barrier, inc=1, device_id=where(peer), device_id_type=MESH)
        return carry

    lax.fori_loop(1, members, greet, 0)
    pl.semaphore_wait(barrier, members - 1)
    locals_ = [
        pltpu.make_async_copy(source(a, me), dsts[a].at[me], local_sems.at[a]) for a in range(count)
    ]
    for local in locals_:
        local.start()

    def send(step, carry):
        peer = lax.rem(me + step, members)
        for a in range(count):
            remote(a, step, peer, peer, me).start()
        return carry

    lax.fori_loop(1, members, send, 0)

    def finish(step, carry):
        peer = lax.rem(me + step, members)
        sender = lax.rem(me + members - step, members)
        for a in range(count):
            remote(a, step, peer, peer, me).wait_send()
            remote(a, step, sender, me, sender).wait_recv()
        return carry

    lax.fori_loop(1, members, finish, 0)
    for local in locals_:
        local.wait()


def exchange(blocks, members, axis, stride, gather, ident):
    count = len(blocks)
    shapes = [jax.ShapeDtypeStruct((members,) + b.shape[1:], b.dtype) for b in blocks]
    return pl.pallas_call(
        functools.partial(exchange_kernel, members, axis, stride, gather, count),
        out_shape=shapes,
        in_specs=[pl.BlockSpec(memory_space=pl.ANY)] * count,
        out_specs=[pl.BlockSpec(memory_space=pl.ANY)] * count,
        scratch_shapes=[
            pltpu.SemaphoreType.DMA((count, members)),
            pltpu.SemaphoreType.DMA((count, members)),
            pltpu.SemaphoreType.DMA((count,)),
        ],
        compiler_params=pltpu.CompilerParams(collective_id=ident, has_side_effects=True),
    )(*blocks)


def reduce_gather_kernel(rows_y, src_ref, out_ref, stage, total, sends, recvs, shares, gets, local_sems):
    coord = lax.axis_index("grp")
    other = lax.axis_index("dev")
    groups = 2 * rows_y
    me = coord // 2
    core = lax.rem(coord, 2)
    barrier = pltpu.get_barrier_semaphore()

    def greet(step, carry):
        peer = lax.rem(coord + step, groups)
        pl.semaphore_signal(barrier, inc=1, device_id=(peer, other), device_id_type=MESH)
        return carry

    lax.fori_loop(1, groups, greet, 0)
    pl.semaphore_wait(barrier, groups - 1)
    own = pltpu.make_async_copy(src_ref.at[me], stage.at[me], local_sems.at[0])
    own.start()

    def scatter(step, peer, src_peer, slot):
        return pltpu.make_async_remote_copy(
            src_ref=src_ref.at[src_peer],
            dst_ref=stage.at[slot],
            send_sem=sends.at[step],
            recv_sem=recvs.at[step],
            device_id=(peer * 2 + core, other),
            device_id_type=MESH,
        )

    def send_part(step, carry):
        peer = lax.rem(me + step, rows_y)
        scatter(step, peer, peer, me).start()
        return carry

    lax.fori_loop(1, rows_y, send_part, 0)

    def finish_part(step, carry):
        peer = lax.rem(me + step, rows_y)
        sender = lax.rem(me + rows_y - step, rows_y)
        scatter(step, peer, peer, me).wait_send()
        scatter(step, sender, me, sender).wait_recv()
        return carry

    lax.fori_loop(1, rows_y, finish_part, 0)
    own.wait()
    total[...] = jnp.sum(stage[...], axis=0)
    mine = pltpu.make_async_copy(total, out_ref.at[coord], local_sems.at[1])
    mine.start()

    def spread(step, peer, slot):
        return pltpu.make_async_remote_copy(
            src_ref=total,
            dst_ref=out_ref.at[slot],
            send_sem=shares.at[step],
            recv_sem=gets.at[step],
            device_id=(peer, other),
            device_id_type=MESH,
        )

    def send_total(step, carry):
        spread(step, lax.rem(coord + step, groups), coord).start()
        return carry

    lax.fori_loop(1, groups, send_total, 0)

    def finish_total(step, carry):
        spread(step, lax.rem(coord + step, groups), coord).wait_send()
        sender = lax.rem(coord + groups - step, groups)
        spread(step, sender, sender).wait_recv()
        return carry

    lax.fori_loop(1, groups, finish_total, 0)
    mine.wait()


def reduce_gather(part, ident):
    rows_y, depth, span = part.shape
    groups = 2 * rows_y
    return pl.pallas_call(
        functools.partial(reduce_gather_kernel, rows_y),
        out_shape=jax.ShapeDtypeStruct((groups, depth, span), part.dtype),
        in_specs=[pl.BlockSpec(memory_space=pl.ANY)],
        out_specs=pl.BlockSpec(memory_space=pl.ANY),
        scratch_shapes=[
            pltpu.VMEM((rows_y, depth, span), part.dtype),
            pltpu.VMEM((depth, span), part.dtype),
            pltpu.SemaphoreType.DMA((rows_y,)),
            pltpu.SemaphoreType.DMA((rows_y,)),
            pltpu.SemaphoreType.DMA((groups,)),
            pltpu.SemaphoreType.DMA((groups,)),
            pltpu.SemaphoreType.DMA((2,)),
        ],
        compiler_params=pltpu.CompilerParams(collective_id=ident, has_side_effects=True),
    )(part)


def gelu_slope(value):
    return (
        0.5 * (1.0 + lax.erf(value * 0.7071067811865476))
        + value * jnp.exp(-0.5 * value * value) * 0.3989422804014327
    )


def slope_from(value, cdf):
    return cdf + value * jnp.exp(-0.5 * value * value) * 0.3989422804014327


def local_pass(wave, lens, w_first, norm_gain, norm_bias, w_second, cot):
    rows, samp = wave.shape
    ker_first = w_first.shape[0]
    stride_first = ker_first // 2
    chans = w_first.shape[1]
    taps_second = w_second.shape[0]
    frames0 = (samp - ker_first) // stride_first + 1
    frames1 = (frames0 - taps_second) // 2 + 1
    pairs = (frames0 + 1) // 2
    hop = 2 * stride_first
    reach = hop + stride_first
    padded = jnp.pad(wave, ((0, 0), (0, hop * (pairs + 1) - samp)))
    blocks = padded.reshape(rows, pairs + 1, hop)
    patches = jnp.concatenate([blocks[:, :-1], blocks[:, 1:, :stride_first]], axis=2)
    zeros_w = jnp.zeros((stride_first, chans), w_first.dtype)
    w_pair = jnp.concatenate(
        [
            jnp.concatenate([w_first, zeros_w], axis=0),
            jnp.concatenate([zeros_w, w_first], axis=0),
        ],
        axis=1,
    )
    pre0 = jnp.einsum("rum,mc->ruc", patches, w_pair, preferred_element_type=jnp.float32)
    valid0 = (lens - ker_first) // stride_first + 1
    frame = (
        2 * jnp.arange(pairs, dtype=jnp.int32)[:, None]
        + (jnp.arange(2 * chans, dtype=jnp.int32) // chans)[None, :]
    )
    mask0 = (frame[None] < valid0[:, None, None]).astype(jnp.float32)
    count0 = valid0.astype(jnp.float32)[:, None]

    def fold(x):
        s = jnp.sum(x, axis=1)
        return s[:, :chans] + s[:, chans:]

    def spread(x):
        return jnp.concatenate([x, x], axis=1)[:, None, :]

    mean0 = fold(pre0 * mask0) / count0
    centred = (pre0 - spread(mean0)) * mask0
    var0 = fold(centred * centred) / count0
    inv_std = spread(lax.rsqrt(var0 + 1e-05))
    normed = centred * inv_std
    gain2 = jnp.concatenate([norm_gain, norm_gain])
    bias2 = jnp.concatenate([norm_bias, norm_bias])
    lifted = normed * gain2 + bias2
    cdf0 = 0.5 * (1.0 + lax.erf(lifted * 0.7071067811865476))
    act0 = (lifted * cdf0 * mask0).astype(jnp.bfloat16)
    taps = jnp.concatenate([act0[:, :frames1], act0[:, 1 : frames1 + 1, :chans]], axis=2)
    kernel = w_second.reshape(taps_second * chans, chans)
    pre1 = jnp.einsum("rui,io->ruo", taps, kernel, preferred_element_type=jnp.float32)
    valid1 = (valid0 - taps_second) // 2 + 1
    mask1 = (jnp.arange(frames1, dtype=jnp.int32)[None, :] < valid1[:, None]).astype(jnp.float32)[
        :, :, None
    ]
    cdf1 = 0.5 * (1.0 + lax.erf(pre1 * 0.7071067811865476))
    features = (pre1 * cdf1 * mask1).astype(jnp.bfloat16)
    grad1 = (cot.astype(jnp.float32) * slope_from(pre1, cdf1) * mask1).astype(jnp.bfloat16)
    members = lax.axis_size("dev")
    width = chans // members
    grad_kernel = jnp.einsum("ruo,rui->oi", grad1, taps, preferred_element_type=jnp.float32)
    grad_kernel = grad_kernel.reshape(members, 2, width // 2, -1).transpose(1, 0, 2, 3)
    back = jnp.einsum("ruo,io->rui", grad1, kernel, preferred_element_type=jnp.float32)
    dact0 = jnp.pad(back[:, :, : 2 * chans], ((0, 0), (0, pairs - frames1), (0, 0))) + jnp.pad(
        back[:, :, 2 * chans :], ((0, 0), (1, pairs - frames1 - 1), (0, chans))
    )
    dlift = dact0 * slope_from(lifted, cdf0) * mask0
    gain_terms = jnp.sum(dlift * normed, axis=(0, 1))
    bias_terms = jnp.sum(dlift, axis=(0, 1))
    grad_gain = gain_terms[:chans] + gain_terms[chans:]
    grad_bias = bias_terms[:chans] + bias_terms[chans:]
    dnorm = dlift * gain2
    first_mean = spread(fold(dnorm) / count0)
    second_mean = spread(fold(dnorm * normed) / count0)
    dpre0 = inv_std * (dnorm - first_mean - normed * second_mean) * mask0
    high = dpre0.astype(jnp.bfloat16)
    low = (dpre0 - high.astype(jnp.float32)).astype(jnp.bfloat16)
    grad_pair = jnp.einsum(
        "ruj,rum->jm", high, patches, preferred_element_type=jnp.float32
    ) + jnp.einsum("ruj,rum->jm", low, patches, preferred_element_type=jnp.float32)
    grad_filter = grad_pair[:chans, :ker_first] + grad_pair[chans:, stride_first:]
    small = jnp.concatenate([grad_filter, grad_gain[:, None], grad_bias[:, None]], axis=1)
    small = small.reshape(members, 2, width // 2, small.shape[1]).transpose(1, 0, 2, 3)
    grads = (grad_kernel, small)
    return (features, grads)


def shards(wave, lengths, order, w_first, norm_gain, norm_bias, w_second, cot):
    members = lax.axis_size("dev")
    member = lax.axis_index("dev")
    rows = wave.shape[0]
    share = rows // members
    own_order = lax.dynamic_index_in_dim(order, member, 0, keepdims=False)
    dealt = own_order.reshape(share, members).T.reshape(rows)
    outgoing = jnp.take(wave, dealt, axis=0)
    (arrived,) = exchange([outgoing.reshape(members, share, -1)], members, "dev", 1, False, 3)
    arrived = arrived.reshape(rows, -1)
    picks = lax.dynamic_index_in_dim(
        order.reshape(members, share, members), member, 2, keepdims=False
    )
    slots = jnp.arange(rows, dtype=jnp.int32)
    hits = picks[:, :, None] == slots[None, None, :]
    lens = jnp.sum(
        jnp.where(hits, lengths.reshape(members, 1, rows), 0), axis=2, dtype=jnp.int32
    ).reshape(rows)
    features, (grad_kernel, small) = local_pass(
        arrived, lens, w_first, norm_gain, norm_bias, w_second, cot
    )
    taps_second = w_second.shape[0]
    in_chans = w_second.shape[1]
    ker_first = w_first.shape[0]
    members = lax.axis_size("dev")
    groups = lax.axis_size("grp")
    core = lax.rem(lax.axis_index("grp"), 2)
    pairs = [(g, g ^ 1) for g in range(groups)]

    def pair_sum(halves):
        keep = lax.dynamic_index_in_dim(halves, core, 0, keepdims=False)
        give = lax.dynamic_index_in_dim(halves, 1 - core, 0, keepdims=False)
        return keep + lax.ppermute(give, "grp", pairs)

    mine_kernel = pair_sum(grad_kernel).astype(jnp.bfloat16)
    mine_small = pair_sum(small)
    rounded = lax.reduce_precision(mine_small, exponent_bits=8, mantissa_bits=7)
    small_high = rounded.astype(jnp.bfloat16)
    small_low = (mine_small - rounded).astype(jnp.bfloat16)
    (pieces,) = exchange(
        [jnp.concatenate([mine_kernel, small_high, small_low], axis=2)], members, "dev", 1, False, 0
    )
    sums = jnp.sum(pieces.astype(jnp.float32), axis=0)
    extra = small.shape[-1]
    lead = sums.shape[1] - 2 * extra
    part = jnp.concatenate(
        [sums[:, :lead], sums[:, lead : lead + extra] + sums[:, lead + extra :]], axis=1
    )
    chans = w_second.shape[2]
    width = chans // members
    span = part.shape[1]
    rows_y = groups // 2
    gathered = reduce_gather(part.reshape(rows_y, (width // 2) // rows_y, span), 1)
    gathered = gathered.reshape(rows_y, 2, (width // 2) // rows_y, span)
    owned = gathered.transpose(1, 0, 2, 3).reshape(width, span)
    grad_second = (
        owned[:, : taps_second * in_chans].reshape(width, taps_second, in_chans).transpose(1, 2, 0)
    )
    grad_first = owned[:, taps_second * in_chans : taps_second * in_chans + ker_first].T
    grad_gain = owned[:, taps_second * in_chans + ker_first]
    grad_bias = owned[:, taps_second * in_chans + ker_first + 1]
    return (features, grad_second, grad_first, grad_gain, grad_bias)


def solution(mesh):
    placed = (
        P(("grp", "dev"), None),
        P("grp"),
        P("grp", None),
        P(),
        P(),
        P(),
        P(),
        P(("grp", "dev"), None, None),
    )
    return jax.shard_map(
        shards,
        mesh=mesh,
        in_specs=placed,
        out_specs=(
            P(("grp", "dev"), None, None),
            P(None, None, "dev"),
            P(None, "dev"),
            P("dev"),
            P("dev"),
        ),
        check_vma=False,
    )
```

```python
import functools

import jax
import jax.numpy as jnp
from jax import lax
from jax.experimental import pallas as pl
from jax.experimental.pallas import tpu as pltpu
from jax.sharding import PartitionSpec as P

MESH = pl.DeviceIdType.MESH


def exchange_kernel(members, axis, stride, gather, count, *refs):
    srcs = refs[:count]
    dsts = refs[count : 2 * count]
    send_sems, recv_sems, local_sems = refs[2 * count :]
    if axis == "grp":
        coord = lax.axis_index("grp")
        me = coord // stride
        offset = lax.rem(coord, stride)
        other = lax.axis_index("dev")
    else:
        me = lax.axis_index("dev")
        other = lax.axis_index("grp")

    def where(peer):
        return (peer * stride + offset, other) if axis == "grp" else (other, peer)

    def source(a, peer):
        return srcs[a].at[0] if gather else srcs[a].at[peer]

    def remote(a, step, peer, src_peer, slot):
        return pltpu.make_async_remote_copy(
            src_ref=source(a, src_peer),
            dst_ref=dsts[a].at[slot],
            send_sem=send_sems.at[a, step],
            recv_sem=recv_sems.at[a, step],
            device_id=where(peer),
            device_id_type=MESH,
        )

    barrier = pltpu.get_barrier_semaphore()

    def greet(step, carry):
        peer = lax.rem(me + step, members)
        pl.semaphore_signal(barrier, inc=1, device_id=where(peer), device_id_type=MESH)
        return carry

    lax.fori_loop(1, members, greet, 0)
    pl.semaphore_wait(barrier, members - 1)
    locals_ = [
        pltpu.make_async_copy(source(a, me), dsts[a].at[me], local_sems.at[a]) for a in range(count)
    ]
    for local in locals_:
        local.start()

    def send(step, carry):
        peer = lax.rem(me + step, members)
        for a in range(count):
            remote(a, step, peer, peer, me).start()
        return carry

    lax.fori_loop(1, members, send, 0)

    def finish(step, carry):
        peer = lax.rem(me + step, members)
        sender = lax.rem(me + members - step, members)
        for a in range(count):
            remote(a, step, peer, peer, me).wait_send()
            remote(a, step, sender, me, sender).wait_recv()
        return carry

    lax.fori_loop(1, members, finish, 0)
    for local in locals_:
        local.wait()


def exchange(blocks, members, axis, stride, gather, ident):
    count = len(blocks)
    shapes = [jax.ShapeDtypeStruct((members,) + b.shape[1:], b.dtype) for b in blocks]
    return pl.pallas_call(
        functools.partial(exchange_kernel, members, axis, stride, gather, count),
        out_shape=shapes,
        in_specs=[pl.BlockSpec(memory_space=pl.ANY)] * count,
        out_specs=[pl.BlockSpec(memory_space=pl.ANY)] * count,
        scratch_shapes=[
            pltpu.SemaphoreType.DMA((count, members)),
            pltpu.SemaphoreType.DMA((count, members)),
            pltpu.SemaphoreType.DMA((count,)),
        ],
        compiler_params=pltpu.CompilerParams(collective_id=ident, has_side_effects=True),
    )(*blocks)


def reduce_gather_kernel(rows_y, src_ref, out_ref, stage, total, sends, recvs, shares, gets, local_sems):
    coord = lax.axis_index("grp")
    other = lax.axis_index("dev")
    groups = 2 * rows_y
    me = coord // 2
    core = lax.rem(coord, 2)
    barrier = pltpu.get_barrier_semaphore()

    def greet(step, carry):
        peer = lax.rem(coord + step, groups)
        pl.semaphore_signal(barrier, inc=1, device_id=(peer, other), device_id_type=MESH)
        return carry

    lax.fori_loop(1, groups, greet, 0)
    pl.semaphore_wait(barrier, groups - 1)
    own = pltpu.make_async_copy(src_ref.at[me], stage.at[me], local_sems.at[0])
    own.start()

    def scatter(step, peer, src_peer, slot):
        return pltpu.make_async_remote_copy(
            src_ref=src_ref.at[src_peer],
            dst_ref=stage.at[slot],
            send_sem=sends.at[step],
            recv_sem=recvs.at[step],
            device_id=(peer * 2 + core, other),
            device_id_type=MESH,
        )

    def send_part(step, carry):
        peer = lax.rem(me + step, rows_y)
        scatter(step, peer, peer, me).start()
        return carry

    lax.fori_loop(1, rows_y, send_part, 0)

    def finish_part(step, carry):
        peer = lax.rem(me + step, rows_y)
        sender = lax.rem(me + rows_y - step, rows_y)
        scatter(step, peer, peer, me).wait_send()
        scatter(step, sender, me, sender).wait_recv()
        return carry

    lax.fori_loop(1, rows_y, finish_part, 0)
    own.wait()
    total[...] = jnp.sum(stage[...], axis=0)
    mine = pltpu.make_async_copy(total, out_ref.at[coord], local_sems.at[1])
    mine.start()

    def spread(step, peer, slot):
        return pltpu.make_async_remote_copy(
            src_ref=total,
            dst_ref=out_ref.at[slot],
            send_sem=shares.at[step],
            recv_sem=gets.at[step],
            device_id=(peer, other),
            device_id_type=MESH,
        )

    def send_total(step, carry):
        spread(step, lax.rem(coord + step, groups), coord).start()
        return carry

    lax.fori_loop(1, groups, send_total, 0)

    def finish_total(step, carry):
        spread(step, lax.rem(coord + step, groups), coord).wait_send()
        sender = lax.rem(coord + groups - step, groups)
        spread(step, sender, sender).wait_recv()
        return carry

    lax.fori_loop(1, groups, finish_total, 0)
    mine.wait()


def reduce_gather(part, ident):
    rows_y, depth, span = part.shape
    groups = 2 * rows_y
    return pl.pallas_call(
        functools.partial(reduce_gather_kernel, rows_y),
        out_shape=jax.ShapeDtypeStruct((groups, depth, span), part.dtype),
        in_specs=[pl.BlockSpec(memory_space=pl.ANY)],
        out_specs=pl.BlockSpec(memory_space=pl.ANY),
        scratch_shapes=[
            pltpu.VMEM((rows_y, depth, span), part.dtype),
            pltpu.VMEM((depth, span), part.dtype),
            pltpu.SemaphoreType.DMA((rows_y,)),
            pltpu.SemaphoreType.DMA((rows_y,)),
            pltpu.SemaphoreType.DMA((groups,)),
            pltpu.SemaphoreType.DMA((groups,)),
            pltpu.SemaphoreType.DMA((2,)),
        ],
        compiler_params=pltpu.CompilerParams(collective_id=ident, has_side_effects=True),
    )(part)


def gelu_slope(value):
    return (
        0.5 * (1.0 + lax.erf(value * 0.7071067811865476))
        + value * jnp.exp(-0.5 * value * value) * 0.3989422804014327
    )


def slope_from(value, cdf):
    return cdf + value * jnp.exp(-0.5 * value * value) * 0.3989422804014327


def local_pass(wave, lens, w_first, norm_gain, norm_bias, w_second, cot):
    rows, samp = wave.shape
    ker_first = w_first.shape[0]
    stride_first = ker_first // 2
    chans = w_first.shape[1]
    taps_second = w_second.shape[0]
    frames0 = (samp - ker_first) // stride_first + 1
    frames1 = (frames0 - taps_second) // 2 + 1
    pairs = (frames0 + 1) // 2
    hop = 2 * stride_first
    reach = hop + stride_first
    padded = jnp.pad(wave, ((0, 0), (0, hop * (pairs + 1) - samp)))
    blocks = padded.reshape(rows, pairs + 1, hop)
    patches = jnp.concatenate([blocks[:, :-1], blocks[:, 1:, :stride_first]], axis=2)
    zeros_w = jnp.zeros((stride_first, chans), w_first.dtype)
    w_pair = jnp.concatenate(
        [
            jnp.concatenate([w_first, zeros_w], axis=0),
            jnp.concatenate([zeros_w, w_first], axis=0),
        ],
        axis=1,
    )
    pre0 = jnp.einsum("rum,mc->ruc", patches, w_pair, preferred_element_type=jnp.float32)
    valid0 = (lens - ker_first) // stride_first + 1
    frame = (
        2 * jnp.arange(pairs, dtype=jnp.int32)[:, None]
        + (jnp.arange(2 * chans, dtype=jnp.int32) // chans)[None, :]
    )
    mask0 = (frame[None] < valid0[:, None, None]).astype(jnp.float32)
    count0 = valid0.astype(jnp.float32)[:, None]

    def fold(x):
        s = jnp.sum(x, axis=1)
        return s[:, :chans] + s[:, chans:]

    def spread(x):
        return jnp.concatenate([x, x], axis=1)[:, None, :]

    mean0 = fold(pre0 * mask0) / count0
    centred = (pre0 - spread(mean0)) * mask0
    var0 = fold(centred * centred) / count0
    inv_std = spread(lax.rsqrt(var0 + 1e-05))
    normed = centred * inv_std
    gain2 = jnp.concatenate([norm_gain, norm_gain])
    bias2 = jnp.concatenate([norm_bias, norm_bias])
    lifted = normed * gain2 + bias2
    cdf0 = 0.5 * (1.0 + lax.erf(lifted * 0.7071067811865476))
    act0 = (lifted * cdf0 * mask0).astype(jnp.bfloat16)
    taps = jnp.concatenate([act0[:, :frames1], act0[:, 1 : frames1 + 1, :chans]], axis=2)
    kernel = w_second.reshape(taps_second * chans, chans)
    pre1 = jnp.einsum("rui,io->ruo", taps, kernel, preferred_element_type=jnp.float32)
    valid1 = (valid0 - taps_second) // 2 + 1
    mask1 = (jnp.arange(frames1, dtype=jnp.int32)[None, :] < valid1[:, None]).astype(jnp.float32)[
        :, :, None
    ]
    cdf1 = 0.5 * (1.0 + lax.erf(pre1 * 0.7071067811865476))
    features = (pre1 * cdf1 * mask1).astype(jnp.bfloat16)
    grad1 = (cot.astype(jnp.float32) * slope_from(pre1, cdf1) * mask1).astype(jnp.bfloat16)
    members = lax.axis_size("dev")
    width = chans // members
    grad_kernel = jnp.einsum("ruo,rui->oi", grad1, taps, preferred_element_type=jnp.float32)
    grad_kernel = grad_kernel.reshape(members, 2, width // 2, -1).transpose(1, 0, 2, 3)
    back = jnp.einsum("ruo,io->rui", grad1, kernel, preferred_element_type=jnp.float32)
    dact0 = jnp.pad(back[:, :, : 2 * chans], ((0, 0), (0, pairs - frames1), (0, 0))) + jnp.pad(
        back[:, :, 2 * chans :], ((0, 0), (1, pairs - frames1 - 1), (0, chans))
    )
    dlift = dact0 * slope_from(lifted, cdf0) * mask0
    gain_terms = jnp.sum(dlift * normed, axis=(0, 1))
    bias_terms = jnp.sum(dlift, axis=(0, 1))
    grad_gain = gain_terms[:chans] + gain_terms[chans:]
    grad_bias = bias_terms[:chans] + bias_terms[chans:]
    dnorm = dlift * gain2
    first_mean = spread(fold(dnorm) / count0)
    second_mean = spread(fold(dnorm * normed) / count0)
    dpre0 = inv_std * (dnorm - first_mean - normed * second_mean) * mask0
    high = dpre0.astype(jnp.bfloat16)
    low = (dpre0 - high.astype(jnp.float32)).astype(jnp.bfloat16)
    grad_pair = jnp.einsum(
        "ruj,rum->jm", high, patches, preferred_element_type=jnp.float32
    ) + jnp.einsum("ruj,rum->jm", low, patches, preferred_element_type=jnp.float32)
    grad_filter = grad_pair[:chans, :ker_first] + grad_pair[chans:, stride_first:]
    small = jnp.concatenate([grad_filter, grad_gain[:, None], grad_bias[:, None]], axis=1)
    small = small.reshape(members, 2, width // 2, small.shape[1]).transpose(1, 0, 2, 3)
    grads = (grad_kernel, small)
    return (features, grads)


def shards(wave, lengths, order, w_first, norm_gain, norm_bias, w_second, cot):
    members = lax.axis_size("dev")
    member = lax.axis_index("dev")
    rows = wave.shape[0]
    share = rows // members
    own_order = lax.dynamic_index_in_dim(order, member, 0, keepdims=False)
    dealt = own_order.reshape(share, members).T.reshape(rows)
    chooser = (dealt[:, None] == jnp.arange(rows, dtype=jnp.int32)[None, :]).astype(wave.dtype)
    outgoing = jnp.dot(chooser, wave, preferred_element_type=jnp.float32).astype(wave.dtype)
    (arrived,) = exchange([outgoing.reshape(members, share, -1)], members, "dev", 1, False, 3)
    arrived = arrived.reshape(rows, -1)
    picks = lax.dynamic_index_in_dim(
        order.reshape(members, share, members), member, 2, keepdims=False
    )
    slots = jnp.arange(rows, dtype=jnp.int32)
    hits = picks[:, :, None] == slots[None, None, :]
    lens = jnp.sum(
        jnp.where(hits, lengths.reshape(members, 1, rows), 0), axis=2, dtype=jnp.int32
    ).reshape(rows)
    features, (grad_kernel, small) = local_pass(
        arrived, lens, w_first, norm_gain, norm_bias, w_second, cot
    )
    taps_second = w_second.shape[0]
    in_chans = w_second.shape[1]
    ker_first = w_first.shape[0]
    members = lax.axis_size("dev")
    groups = lax.axis_size("grp")
    core = lax.rem(lax.axis_index("grp"), 2)
    pairs = [(g, g ^ 1) for g in range(groups)]

    def pair_sum(halves):
        keep = lax.dynamic_index_in_dim(halves, core, 0, keepdims=False)
        give = lax.dynamic_index_in_dim(halves, 1 - core, 0, keepdims=False)
        return keep + lax.ppermute(give, "grp", pairs)

    mine_kernel = pair_sum(grad_kernel).astype(jnp.bfloat16)
    mine_small = pair_sum(small)
    rounded = lax.reduce_precision(mine_small, exponent_bits=8, mantissa_bits=7)
    small_high = rounded.astype(jnp.bfloat16)
    small_low = (mine_small - rounded).astype(jnp.bfloat16)
    (pieces,) = exchange(
        [jnp.concatenate([mine_kernel, small_high, small_low], axis=2)], members, "dev", 1, False, 0
    )
    sums = jnp.sum(pieces.astype(jnp.float32), axis=0)
    extra = small.shape[-1]
    lead = sums.shape[1] - 2 * extra
    part = jnp.concatenate(
        [sums[:, :lead], sums[:, lead : lead + extra] + sums[:, lead + extra :]], axis=1
    )
    chans = w_second.shape[2]
    width = chans // members
    span = part.shape[1]
    rows_y = groups // 2
    gathered = reduce_gather(part.reshape(rows_y, (width // 2) // rows_y, span), 1)
    gathered = gathered.reshape(rows_y, 2, (width // 2) // rows_y, span)
    owned = gathered.transpose(1, 0, 2, 3).reshape(width, span)
    grad_second = (
        owned[:, : taps_second * in_chans].reshape(width, taps_second, in_chans).transpose(1, 2, 0)
    )
    grad_first = owned[:, taps_second * in_chans : taps_second * in_chans + ker_first].T
    grad_gain = owned[:, taps_second * in_chans + ker_first]
    grad_bias = owned[:, taps_second * in_chans + ker_first + 1]
    return (features, grad_second, grad_first, grad_gain, grad_bias)


def solution(mesh):
    placed = (
        P(("grp", "dev"), None),
        P("grp"),
        P("grp", None),
        P(),
        P(),
        P(),
        P(),
        P(("grp", "dev"), None, None),
    )
    return jax.shard_map(
        shards,
        mesh=mesh,
        in_specs=placed,
        out_specs=(
            P(("grp", "dev"), None, None),
            P(None, None, "dev"),
            P(None, "dev"),
            P("dev"),
            P("dev"),
        ),
        check_vma=False,
    )
```
